32 devices in a mesh: parts: 2 (over y), tp: 16 (over z, x, core).
Axes of the slice: x: 2, y: 2, z: 4, core: 2. Of those that a mesh axis runs over, the one named last changes fastest.
Arguments:
- embeddings: bfloat16 [2, 3, 96, 4096], P('parts'), parts along dimension 0, may hold values from -6 to 6
- lengths: int32 [2, 3], P('parts'), parts along dimension 0, may hold values from 1 to 96, 192 in all within a row
- mem_init: bfloat16 [4, 32, 4096], replicated, may hold values from -6 to 6
- norm_gain: float32 [4, 4096], replicated, may hold values from 0.1 to 1.9
- w_query: bfloat16 [4096, 16384], P(None, 'tp'), as said below
- w_key: bfloat16 [4096, 4096], P(None, 'tp'), as said below
- w_value: bfloat16 [4096, 4096], P(None, 'tp'), may hold values from -0.09375 to 0.09375
- w_out: bfloat16 [16384, 4096], P('tp'), may hold values from -0.25 to 0.25
Outputs:
- layer_states: bfloat16 [16, 6, 32, 4096], P('tp', 'parts'), parts along dimension 1
The draws below stay inside these ranges and needn't reach their ends.
There are 2 independent parts, one for each index of `parts`. The reference program is written for one: setup_inputs(seed, part) draws one part's arguments, and reference() takes and returns one part's arrays. A program takes and returns all parts, laid end to end along the dimension named above; an argument that names none is the same for every part. Nothing has to cross between parts.
Inputs may be any that keep to these rules, and one draw needn't show every extreme that they name: Segment k of sequence s holds lengths[s, k] real tokens in its first slots; the lengths of one sequence sum to 192 and one of them is 96. `w_query`: weights of order D ** -0.5 for each entry. `w_key`: weights of order D ** -0.5 for each entry.
All inputs are finite; a program needn't handle non-finite values.
Results may differ from the reference program's by a relative error of at most 0.039.
Values may be sent and summed in bfloat16 or wider, within the bound.
A program may use at most 128 MiB of HBM per device.

```python
import math
import jax
import jax.numpy as jnp
import numpy as np
from jax import lax

D = 4096
HEADS = 32
KVH = 8
HD = 128
MEM = 32
SECTIONS = 4
SEGS = 3
SEG = 96
TPW = 4
SEQS = 1


def key_matrix(key):
    return jax.random.normal(jax.random.fold_in(key, 71), (D, SECTIONS * KVH * HD), jnp.float32) * D ** (-0.5)


def draw_w_key(key, part):
    return key_matrix(key).astype(jnp.bfloat16)


def draw_w_query(key, part):
    normal_part = jax.random.normal(jax.random.fold_in(key, 72), (D, SECTIONS * HEADS * HD), jnp.float32) * D ** (-0.5)
    return normal_part.astype(jnp.bfloat16)


def steps_of(stream_key, dims, shards, least, high):
    factor_of, own = 1.0, jax.random.fold_in(stream_key, 6)
    for position, blocks in shards:
        draws = jnp.exp(jax.random.uniform(jax.random.fold_in(own, position), (blocks,), jnp.float32, least / len(shards), high / len(shards)))
        factor_of = factor_of * jnp.repeat(draws, dims[position] // blocks).reshape([-1 if axis == position else 1 for axis in range(len(dims))])
    return factor_of


def length_profile(count, total, limit, lean):
    portions = [(1 << 20) // math.isqrt(grade ** lean) + 1 for grade in range(2, count + 1)]
    surplus, counts = total - limit - (count - 1), [1] * (count - 1)
    while surplus > 0:
        movable = [i for i in range(count - 1) if counts[i] < limit]
        mass, left = sum([portions[i] for i in movable]), surplus
        for i in movable:
            extra = min(limit - counts[i], max(1, left * portions[i] // mass), surplus)
            counts[i] = counts[i] + extra
            surplus = surplus - extra
    return np.array([limit] + counts)


def uneven_parts(own_key, amount, total, most, lean):
    if amount == 2:
        one = jax.random.randint(own_key, (), max(1, total - most), min(most, total - 1) + 1)
        return jnp.stack([one, total - one])
    sizes = jnp.asarray(length_profile(amount, total, most, lean), jnp.int32)
    couples = (amount - 1) // 2
    giver, sink = sizes[1:1 + 2 * couples:2], sizes[2:2 + 2 * couples:2]
    room = jnp.minimum(giver - 1, most - sink)
    moved = jax.random.randint(jax.random.fold_in(own_key, 1), (couples,), 0, 1 << 20) % (room + 1)
    sizes = sizes.at[1:1 + 2 * couples:2].set(giver - moved).at[2:2 + 2 * couples:2].set(sink + moved)
    return sizes[jax.random.permutation(jax.random.fold_in(own_key, 2), amount)]


def noise(rng, extent, spread, reach, cuts=(), held_as=jnp.bfloat16):
    drawn = jax.random.normal(rng, extent, jnp.float32) * spread
    if len(cuts) > 0:
        drawn = steps_of(rng, extent, cuts, -0.22, 0.18) * drawn
    return jnp.clip(drawn, min=-reach, max=reach).astype(held_as)


def setup_inputs(seed: int = 0, part: int = 0) -> dict:
    splits = jax.random.split(jax.random.key(seed), 9)
    part_keys = jax.random.split(jax.random.fold_in(splits[8], part), 9)
    embeddings = noise(part_keys[0], (SEQS, SEGS, SEG, D), 1.0, 6.0)
    lengths = jax.vmap(lambda own: uneven_parts(own, SEGS, 2 * SEG, SEG, 0))(jax.random.split(part_keys[1], SEQS)).reshape((SEQS, SEGS)).astype(jnp.int32)
    mem_init = noise(splits[2], (SECTIONS, MEM, D), 1.0, 6.0)
    norm_gain = jnp.clip(1.0 + 0.18 * jax.random.normal(splits[3], (SECTIONS, D), jnp.float32), 0.1, 1.9)
    w_query = draw_w_query(jax.random.fold_in(splits[8], 71), part)
    w_key = draw_w_key(jax.random.fold_in(splits[8], 71), part)
    w_value = noise(splits[6], (D, SECTIONS * KVH * HD), D ** -0.5, 0.09375, ((1, 16),))
    w_out = noise(splits[7], (SECTIONS * HEADS * HD, D), (4 * HD) ** -0.5, 0.25, ((0, 16),))
    return {"embeddings": embeddings, "lengths": lengths, "mem_init": mem_init, "norm_gain": norm_gain, "w_query": w_query, "w_key": w_key, "w_value": w_value, "w_out": w_out}


eps = 1e-05
rope_base = 500000.0

def rotate(heads_in):
    row_total = heads_in.shape[0]
    half_size = heads_in.shape[-1] // 2
    frequency = rope_base ** (-(jnp.arange(half_size, dtype=jnp.float32) * 2.0) / heads_in.shape[-1])
    angles = jnp.arange(row_total, dtype=jnp.float32)[:, None] * frequency[None, :]
    cosine = jnp.cos(angles)[:, None, :]
    sine_part = jnp.sin(angles)[:, None, :]
    first_half = heads_in[..., :half_size]
    second_half = heads_in[..., half_size:]
    return jnp.concatenate([first_half * cosine - second_half * sine_part, second_half * cosine + first_half * sine_part], axis=-1)

def visible(row_total, length):
    query_ids = jnp.arange(row_total, dtype=jnp.int32)[:, None]
    key_ids = jnp.arange(row_total, dtype=jnp.int32)[None, :]
    real_key = (key_ids < MEM) | (key_ids - MEM < length)
    ordered = (key_ids <= query_ids) | (query_ids < MEM)
    return real_key & ordered

def normalize(widened, gain_row):
    scaled = widened * lax.rsqrt(lax.optimization_barrier(jnp.mean(widened * widened, axis=-1, keepdims=True)) + eps)
    return (scaled * gain_row).astype(jnp.bfloat16)

def attend(queries, key_heads, values, length):
    row_total = queries.shape[0]
    scores = jnp.einsum('qhd,khd->hqk', queries.astype(jnp.float32), key_heads.astype(jnp.float32)) * HD ** (-0.5)
    scores = jnp.where(visible(row_total, length)[None], scores, -1e+30)
    softmaxed = jax.nn.softmax(scores, axis=-1).astype(jnp.bfloat16)
    return jnp.einsum('hqk,khd->qhd', softmaxed.astype(jnp.float32), values.astype(jnp.float32)).astype(jnp.bfloat16)

def finish(widened, summed_out, length, row_ids):
    new_state = (widened + summed_out).astype(jnp.bfloat16)
    kept_rows = (row_ids < MEM) | (row_ids - MEM < length)
    return jnp.where(kept_rows[:, None], new_state, jnp.zeros_like(new_state))

def reference(embeddings, lengths, mem_init, norm_gain, w_query, w_key, w_value, w_out):
    row_total = SEG + MEM
    row_ids = jnp.arange(row_total, dtype=jnp.int32)
    query_cols = HEADS * HD
    key_cols = KVH * HD
    block_rows = row_total // TPW
    carried = [[embeddings[seq_index, segment] for segment in range(SEGS)] for seq_index in range(SEQS)]
    layer_blocks = []
    for group_index in range(SECTIONS):
        query_weight = w_query[:, group_index * query_cols:(group_index + 1) * query_cols]
        key_weight = w_key[:, group_index * key_cols:(group_index + 1) * key_cols]
        value_weight = w_value[:, group_index * key_cols:(group_index + 1) * key_cols]
        out_weight = w_out[group_index * query_cols:(group_index + 1) * query_cols, :]
        per_sequence = []
        for seq_index in range(SEQS):
            memory = mem_init[group_index]
            outputs = []
            for segment in range(SEGS):
                length = lengths[seq_index, segment]
                inputs = jnp.concatenate([memory, carried[seq_index][segment]], axis=0)
                widened = inputs.astype(jnp.float32)
                normed = normalize(widened, norm_gain[group_index])
                queries = rotate(jnp.dot(normed, query_weight, preferred_element_type=jnp.float32).reshape(row_total, HEADS, HD)).astype(jnp.bfloat16)
                key_raw = lax.optimization_barrier(jnp.dot(normed, key_weight, preferred_element_type=jnp.float32).astype(jnp.bfloat16))
                key_heads = rotate(key_raw.astype(jnp.float32).reshape(row_total, KVH, HD)).astype(jnp.bfloat16)
                values = jnp.dot(normed, value_weight, preferred_element_type=jnp.float32).astype(jnp.bfloat16).reshape(row_total, KVH, HD)
                key_heads = jnp.repeat(key_heads, HEADS // KVH, axis=1)
                values = jnp.repeat(values, HEADS // KVH, axis=1)
                mixed_heads = attend(queries, key_heads, values, length).reshape(row_total, query_cols)
                summed_out = jnp.dot(mixed_heads, out_weight, preferred_element_type=jnp.float32)
                new_state = finish(widened, summed_out, length, row_ids)
                memory_part = new_state[:MEM].reshape(TPW, MEM // TPW, D)
                token_part = new_state[MEM:].reshape(TPW, SEG // TPW, D)
                outputs.append(jnp.concatenate([memory_part, token_part], axis=1))
                memory = new_state[:MEM]
                carried[seq_index][segment] = new_state[MEM:]
            per_sequence.append(jnp.stack(outputs, axis=0))
        stacked = jnp.stack(per_sequence, axis=0)
        layer_blocks.append(jnp.transpose(stacked, (2, 0, 1, 3, 4)).reshape(TPW * SEQS, SEGS, block_rows, D))
    return jnp.concatenate(layer_blocks, axis=0)
```

```python
import jax
import jax.numpy as jnp
import numpy as np
from jax import lax
from jax.experimental import pallas as pl
from jax.experimental.pallas import tpu as pltpu
from jax.sharding import PartitionSpec as P

HD = 128
MEM = 32
SECTIONS = 4
SEGS = 3
SEG = 96


eps = 1e-05
rope_base = 500000.0


def from_partner(block, axis, bit):
    count = lax.axis_size(axis)
    route = []
    for low in range(count):
        high = low | 1 << bit
        if high != low and high < count:
            route += [(low, high), (high, low)]
    return lax.ppermute(block, axis, route)


def shortened(value):
    return jax.tree.map(lambda a: a.astype(jnp.bfloat16) if a.dtype == jnp.float32 else a, value)


def shifted(value, axis, by):
    peers = lax.axis_size(axis)
    pairs = [(i, i + by) for i in range(peers) if 0 <= i + by < peers]
    return lax.ppermute(value, axis, pairs)


def rotate(heads_in, positions):
    half_size = heads_in.shape[-1] // 2
    frequency = rope_base ** (
        -(jnp.arange(half_size, dtype=jnp.float32) * 2.0) / heads_in.shape[-1]
    )
    angles = positions.astype(jnp.float32)[:, None] * frequency[None, :]
    cosine = jnp.cos(angles)[:, None, :]
    sine_part = jnp.sin(angles)[:, None, :]
    first_half = heads_in[..., :half_size]
    second_half = heads_in[..., half_size:]
    return jnp.concatenate(
        [
            first_half * cosine - second_half * sine_part,
            second_half * cosine + first_half * sine_part,
        ],
        axis=-1,
    )


def visible(positions, length):
    query_ids = positions[:, None]
    key_ids = positions[None, :]
    real_key = (key_ids < MEM) | (key_ids - MEM < length)
    ordered = (key_ids <= query_ids) | (query_ids < MEM)
    return real_key & ordered


def normalize(widened, gain_row):
    scaled = widened * lax.rsqrt(jnp.mean(widened * widened, axis=-1, keepdims=True) + eps)
    return (scaled * gain_row).astype(jnp.bfloat16)


def attend(queries, key_heads, value_heads, positions, length):
    row_total = queries.shape[0]
    kv_local = key_heads.shape[1]
    grouped = queries.reshape(row_total, kv_local, -1, queries.shape[-1])
    scores = jnp.einsum(
        "qgrd,kgd->grqk", grouped, key_heads, preferred_element_type=jnp.float32
    ) * HD ** (-0.5)
    scores = jnp.where(visible(positions, length)[None, None], scores, -1e30)
    softmaxed = jax.nn.softmax(scores, axis=-1).astype(jnp.bfloat16)
    mixed = jnp.einsum(
        "grqk,kgd->qgrd", softmaxed, value_heads, preferred_element_type=jnp.float32
    ).astype(jnp.bfloat16)
    return mixed.reshape(row_total, -1)


def finish(widened, summed_out, length, row_ids):
    new_state = (widened + summed_out).astype(jnp.bfloat16)
    kept_rows = (row_ids < MEM) | (row_ids - MEM < length)
    return jnp.where(kept_rows[:, None], new_state, jnp.zeros_like(new_state))


def order_pair(mine, partner, lower_half):
    first_part = jnp.where(lower_half, mine, partner)
    second_part = jnp.where(lower_half, partner, mine)
    return jnp.concatenate([first_part, second_part], axis=0)


def gather_rows(piece, my_rank, seq_bits, rank_bits, level_list):
    stacked = piece
    for rank_bit in level_list:
        partner = from_partner(stacked, "tp", seq_bits + rank_bit)
        upper_half = my_rank // 2**rank_bit % 2 == 1
        stacked = jnp.where(
            upper_half, jnp.stack([partner, stacked], axis=0), jnp.stack([stacked, partner], axis=0)
        )
    axis_bits = list(reversed(level_list))
    order_axes = [axis_bits.index(rank_bit) for rank_bit in reversed(range(rank_bits))]
    stacked = jnp.transpose(stacked, order_axes + [rank_bits, rank_bits + 1])
    return stacked.reshape(2**rank_bits * piece.shape[0], piece.shape[-1])


def scatter_rows(partial_term, my_rank, seq_bits, rank_bits, level_list, shard_rows):
    model_width = partial_term.shape[-1]
    running = partial_term.reshape((2,) * rank_bits + (shard_rows, model_width))
    axis_bits = list(reversed(range(rank_bits)))
    for rank_bit in level_list:
        position = axis_bits.index(rank_bit)
        upper_half = my_rank // 2**rank_bit % 2 == 1
        low_part = lax.index_in_dim(running, 0, position, keepdims=False)
        high_part = lax.index_in_dim(running, 1, position, keepdims=False)
        kept_rows = jnp.where(upper_half, high_part, low_part)
        sent_rows = jnp.where(upper_half, low_part, high_part)
        running = kept_rows + from_partner(
            sent_rows.astype(jnp.bfloat16), "tp", seq_bits + rank_bit
        ).astype(sent_rows.dtype)
        axis_bits = [other_bit for other_bit in axis_bits if other_bit != rank_bit]
    return running


def local(embeddings, lengths, mem_init, norm_gain, w_query, w_key, w_value, w_out):
    axis_width = lax.axis_size("tp")
    group_size = axis_width // SECTIONS
    rank_count = min(8, group_size)
    seq_count = group_size // rank_count
    seq_bits = seq_count.bit_length() - 1
    rank_bits = rank_count.bit_length() - 1
    device_index = lax.axis_index("tp")
    group_index = device_index // group_size
    my_rank = device_index % group_size // seq_count
    my_seq = device_index % seq_count
    model_width = embeddings.shape[-1]
    row_total = SEG + MEM
    shard_rows = row_total // rank_count
    mem_block = MEM // rank_count
    token_block = SEG // rank_count
    within = jnp.arange(shard_rows, dtype=jnp.int32)
    block_ids = jnp.arange(rank_count, dtype=jnp.int32)[:, None]
    positions = jnp.where(
        within[None, :] < mem_block,
        block_ids * mem_block + within[None, :],
        MEM + block_ids * token_block + within[None, :] - mem_block,
    ).reshape(-1)
    row_ids = lax.dynamic_index_in_dim(
        positions.reshape(rank_count, shard_rows), my_rank, 0, keepdims=False
    )
    gain_row = lax.dynamic_index_in_dim(norm_gain, group_index, 0, keepdims=False)
    my_lengths = lax.dynamic_index_in_dim(lengths, my_seq, 0, keepdims=False)
    first_memory = lax.dynamic_slice(
        mem_init, (group_index, my_rank * mem_block, 0), (1, mem_block, model_width)
    ).reshape(mem_block, model_width)
    query_stack, key_stack, value_stack, out_stack = (
        w_query[None],
        w_key[None],
        w_value[None],
        w_out[None],
    )
    for seq_bit in range(seq_bits):
        partner_query, partner_key, partner_value, partner_out = (
            from_partner(shortened(query_stack), "tp", seq_bit).astype(query_stack.dtype),
            from_partner(shortened(key_stack), "tp", seq_bit).astype(key_stack.dtype),
            from_partner(shortened(value_stack), "tp", seq_bit).astype(value_stack.dtype),
            from_partner(shortened(out_stack), "tp", seq_bit).astype(out_stack.dtype),
        )
        lower_half = device_index // 2**seq_bit % 2 == 0
        query_stack = order_pair(query_stack, partner_query, lower_half)
        key_stack = order_pair(key_stack, partner_key, lower_half)
        value_stack = order_pair(value_stack, partner_value, lower_half)
        out_stack = order_pair(out_stack, partner_out, lower_half)
    level_list = list(range(rank_bits))
    states = jnp.zeros((SEGS, shard_rows, model_width), jnp.bfloat16)
    memory = jnp.zeros((mem_block, model_width), jnp.bfloat16)
    arrived = jnp.zeros((token_block, model_width), jnp.bfloat16)
    step_total = SEGS + SECTIONS - 1
    for step_index in range(step_total):
        segment = step_index - group_index
        active = (segment >= 0) & (segment < SEGS)
        clipped = jnp.clip(segment, 0, SEGS - 1)
        length = lax.dynamic_index_in_dim(my_lengths, clipped, 0, keepdims=False)
        embedded = lax.dynamic_slice(
            embeddings,
            (my_seq, clipped, my_rank * token_block, 0),
            (1, 1, token_block, model_width),
        ).reshape(token_block, model_width)
        token_source = jnp.where(group_index == 0, embedded, arrived)
        memory_source = jnp.where(segment == 0, first_memory, memory)
        inputs = jnp.concatenate([memory_source, token_source], axis=0)
        widened = inputs.astype(jnp.float32)
        normed = normalize(widened, gain_row)
        gathered = gather_rows(normed, my_rank, seq_bits, rank_bits, level_list)
        query_all = jnp.einsum(
            "rd,sdc->rsc", gathered, query_stack, preferred_element_type=jnp.float32
        )
        queries = rotate(query_all.reshape(row_total, -1, HD), positions).astype(jnp.bfloat16)
        key_all = jnp.einsum("rd,sdc->rsc", gathered, key_stack, preferred_element_type=jnp.float32)
        key_raw = lax.optimization_barrier(key_all.reshape(row_total, -1).astype(jnp.bfloat16))
        value_all = jnp.einsum(
            "rd,sdc->rsc", gathered, value_stack, preferred_element_type=jnp.float32
        ).astype(jnp.bfloat16)
        key_heads = rotate(
            key_raw.astype(jnp.float32).reshape(row_total, -1, HD), positions
        ).astype(jnp.bfloat16)
        value_heads = value_all.reshape(row_total, -1, HD)
        mixed_heads = attend(queries, key_heads, value_heads, positions, length)
        mixed_split = mixed_heads.reshape(row_total, out_stack.shape[0], out_stack.shape[1])
        partial_term = jnp.einsum(
            "rsc,scd->rd", mixed_split, out_stack, preferred_element_type=jnp.float32
        )
        summed_out = scatter_rows(
            partial_term, my_rank, seq_bits, rank_bits, level_list, shard_rows
        )
        new_state = finish(widened, summed_out, length, row_ids)
        memory = jnp.where(active, new_state[:mem_block], memory)
        states = jnp.where(
            active, lax.dynamic_update_index_in_dim(states, new_state, clipped, 0), states
        )
        if step_index + 1 < step_total:
            arrived = shifted(new_state[mem_block:], "tp", group_size)
    return states[None]


RANKS = 4
CHUNKS = 4
ROWS = SEG + MEM
HALF_TOKENS = SEG // 2
MESH = pl.DeviceIdType.MESH


def rope_tables(head):
    half = head // 2
    frequency = rope_base ** (-(np.arange(half, dtype=np.float64) * 2.0) / head)
    angles = np.arange(ROWS)[:, None] * frequency[None, :]
    cosine, sine = np.cos(angles), np.sin(angles)
    return (
        np.concatenate([cosine, cosine], axis=1).astype(np.float32),
        np.concatenate([-sine, sine], axis=1).astype(np.float32),
    )


def layer_kernel(
    len_ref, gain_ref, cos_ref, sin_ref, m0_ref, emb_ref, wq_ref, wk_ref, wv_ref, wo_ref,
    out_ref,
    wq_v, wk_v, wv_v, wo_v, xin, core_snd, core_rcv, tok_snd, tok_rcv, mem_snd, mem_rcv, newt,
    part, acc, mixed,
    msem, esem, wsem, osem, send_sem, recv_sem,
):
    width = xin.shape[-1]
    half = width // 2
    cw = half // CHUNKS
    q_cols, kv_cols = wq_v.shape[1], wk_v.shape[1]
    me = lax.axis_index("tp")
    group, rank = me // RANKS, me % RANKS
    xb, cb = rank // 2, rank % 2
    core_peer = group * RANKS + xb * 2 + (1 - cb)
    x_peer = group * RANKS + (1 - xb) * 2 + cb
    has_next, has_prev = group < SECTIONS - 1, group > 0
    next_peer, prev_peer = me + RANKS, me - RANKS
    own_rows = pl.ds(pl.multiple_of(MEM + xb * HALF_TOKENS, 16), HALF_TOKENS)
    far_rows = pl.ds(pl.multiple_of(MEM + (1 - xb) * HALF_TOKENS, 16), HALF_TOKENS)
    mem_rows = pl.ds(0, MEM)

    def own_cols(j):
        return pl.ds(pl.multiple_of(cb * half + j * cw, 128), cw)

    def peer_cols(j):
        return pl.ds(pl.multiple_of((1 - cb) * half + j * cw, 128), cw)

    def half_cols(j):
        return pl.ds(j * cw, cw)

    def side_cols(side, j):
        return own_cols(j) if side == 0 else peer_cols(j)

    order = [(0, 0)]
    for j in range(1, CHUNKS):
        order += [(0, j), (1, j - 1)]
    order += [(1, CHUNKS - 1)]

    def weight_copies(o):
        cols = side_cols(*order[o])
        return [
            pltpu.make_async_copy(src.at[cols], dst.at[cols], wsem.at[i, o])
            for i, (src, dst) in enumerate(((wq_ref, wq_v), (wk_ref, wk_v), (wv_ref, wv_v)))
        ]

    def out_copy(side, j):
        cols = side_cols(side, j)
        return pltpu.make_async_copy(wo_ref.at[:, cols], wo_v.at[:, cols], osem.at[side, j])

    def in_copy(k):
        return pltpu.make_async_copy(
            emb_ref.at[0, k], xin.at[k, pl.ds(MEM, SEG)], esem.at[k]
        )

    def remote(src, dst, kind, k, j, peer):
        return pltpu.make_async_remote_copy(
            src_ref=src, dst_ref=dst, send_sem=send_sem.at[kind, k, j],
            recv_sem=recv_sem.at[kind, k, j],
            device_id={"tp": peer}, device_id_type=MESH,
        )

    def in_place(ref, kind, k, j, peer):
        return remote(ref, ref, kind, k, j, peer)

    def z_copy(k, j):
        return remote(
            newt.at[k, :, own_cols(j)], xin.at[k, own_rows, own_cols(j)], 0, k, j, next_peer
        )

    def gather_x(k, j):
        return in_place(xin.at[k, own_rows, own_cols(j)], 1, k, j, x_peer)

    def gather_core(k, j):
        return in_place(xin.at[k, own_rows, own_cols(j)], 2, k, j, core_peer)

    def gather_far(k, j):
        return in_place(xin.at[k, far_rows, own_cols(j)], 3, k, j, core_peer)

    def sum_core(k, j):
        return remote(
            core_snd.at[k, :, half_cols(j)], core_rcv.at[k, :, half_cols(j)], 4, k, j, core_peer
        )

    def sum_tokens(k, j):
        return remote(
            tok_snd.at[k, :, half_cols(j)], tok_rcv.at[k, :, half_cols(j)], 5, k, j, x_peer
        )

    def sum_memory(k, j):
        return remote(
            mem_snd.at[k, :, half_cols(j)], mem_rcv.at[k, :, half_cols(j)], 6, k, j, x_peer
        )

    def next_memory(k, j):
        return in_place(xin.at[k + 1, mem_rows, own_cols(j)], 7, k, j, core_peer)

    def out_tokens(k, j):
        return in_place(newt.at[k, :, own_cols(j)], 8, k, j, core_peer)

    first_memory = pltpu.make_async_copy(m0_ref.at[group], xin.at[0, mem_rows], msem)
    first_memory.start()

    def start_weights(o):
        for copy in weight_copies(o):
            copy.start()

    @pl.when(group == 0)
    def _():
        in_copy(0).start()

    for o in range(2 * CHUNKS):
        start_weights(o)
    for j in range(CHUNKS):
        out_copy(1, j).start()
        out_copy(0, j).start()

    @pl.when(group == 0)
    def _():
        for k in range(1, SEGS):
            in_copy(k).start()

    barrier = pltpu.get_barrier_semaphore()
    for peer in (core_peer, x_peer):
        pl.semaphore_signal(barrier, inc=1, device_id={"tp": peer}, device_id_type=MESH)

    @pl.when(has_next)
    def _():
        pl.semaphore_signal(barrier, inc=1, device_id={"tp": next_peer}, device_id_type=MESH)

    @pl.when(has_prev)
    def _():
        pl.semaphore_signal(barrier, inc=1, device_id={"tp": prev_peer}, device_id_type=MESH)

    inner = has_next & has_prev

    @pl.when(inner)
    def _():
        pl.semaphore_wait(barrier, 4)

    @pl.when(jnp.logical_not(inner))
    def _():
        pl.semaphore_wait(barrier, 3)

    first_memory.wait()

    def pass_on(k, j):
        @pl.when(has_prev)
        def _():
            z_copy(k, j).wait_recv()
            gather_x(k, j).start()
            gather_core(k, j).start()

    def pass_far(k, j):
        @pl.when(has_prev)
        def _():
            gather_x(k, j).wait_recv()
            gather_far(k, j).start()

    def rope(block):
        return block * cos_ref[...] + pltpu.roll(block, HD // 2, 1) * sin_ref[...]

    def emit_out(k):
        length = len_ref[0, k]
        row = lax.broadcasted_iota(jnp.int32, (32, cw), 0)
        kept = (row < 8) | (xb * HALF_TOKENS + cb * 24 + row - 8 < length)
        for j in range(2 * CHUNKS):
            cols = pl.ds(j * cw, cw)
            memory = xin[k + 1, mem_rows, cols].astype(jnp.float32)
            tokens = newt[k, :, cols].astype(jnp.float32)
            low = jnp.where(xb == 0, memory[:16], memory[16:])
            block = jnp.concatenate(
                [
                    jnp.where(cb == 0, low[:8], low[8:]),
                    jnp.where(cb == 0, tokens[:24], tokens[24:]),
                ],
                axis=0,
            )
            out_ref[0, k, :, cols] = jnp.where(kept, block, 0.0).astype(jnp.bfloat16)

    def segment(k, carry):
        length = len_ref[0, k]
        squares = jnp.zeros((ROWS, 1), jnp.float32)
        pass_on(k, 0)
        pass_on(k, 1)

        @pl.when(group == 0)
        def _():
            in_copy(k).wait()

        for o, (side, j) in enumerate(order):
            if side == 0:
                if j + 2 < CHUNKS:
                    pass_on(k, j + 2)
                pass_far(k, j)
            else:

                @pl.when(has_prev)
                def _():
                    gather_core(k, j).wait_recv()
                    gather_far(k, j).wait_recv()

                @pl.when(k > 0)
                def _():
                    next_memory(k - 1, j).wait_recv()

            @pl.when(k == 0)
            def _():
                for copy in weight_copies(o):
                    copy.wait()

            cols = side_cols(side, j)
            raw = xin[k, :, cols].astype(jnp.float32)
            squares = squares + jnp.sum(raw * raw, axis=1, keepdims=True)
            gained = (raw * gain_ref[pl.ds(group, 1), cols]).astype(jnp.bfloat16)
            low = 0
            for weight in (wq_v, wk_v, wv_v):
                high = low + weight.shape[1]
                term = jnp.dot(gained, weight[cols], preferred_element_type=jnp.float32)
                if o == 0:
                    acc[:, low:high] = term
                else:
                    acc[:, low:high] += term
                low = high

        factor = lax.rsqrt(squares * (1.0 / width) + eps)
        query_pos = lax.broadcasted_iota(jnp.int32, (ROWS, ROWS), 0)
        key_pos = lax.broadcasted_iota(jnp.int32, (ROWS, ROWS), 1)
        real_key = (key_pos < MEM) | (key_pos - MEM < length)
        ordered = (key_pos <= query_pos) | (query_pos < MEM)
        bias = jnp.where(real_key & ordered, 0.0, -1e30).astype(jnp.float32)
        per_kv = q_cols // kv_cols
        for g in range(kv_cols // HD):
            key_raw = (acc[:, q_cols + g * HD : q_cols + (g + 1) * HD] * factor).astype(
                jnp.bfloat16
            )
            key = rope(key_raw.astype(jnp.float32)).astype(jnp.bfloat16)
            low = q_cols + kv_cols + g * HD
            value = (acc[:, low : low + HD] * factor).astype(jnp.bfloat16)
            heads = range(g * per_kv, (g + 1) * per_kv)
            queries = jnp.concatenate(
                [
                    rope(acc[:, h * HD : (h + 1) * HD] * factor).astype(jnp.bfloat16)
                    for h in heads
                ],
                axis=0,
            )
            scores = lax.dot_general(
                queries, key, (((1,), (1,)), ((), ())), preferred_element_type=jnp.float32
            ) * HD ** (-0.5)
            scores = scores.reshape(per_kv, ROWS, ROWS) + bias[None]
            weight = jnp.exp(scores - jnp.max(scores, axis=2, keepdims=True))
            share = 1.0 / jnp.sum(weight, axis=2, keepdims=True)
            blended = jnp.dot(
                weight.astype(jnp.bfloat16).reshape(per_kv * ROWS, ROWS),
                value,
                preferred_element_type=jnp.float32,
            ).reshape(per_kv, ROWS, HD) * share
            for i, h in enumerate(heads):
                mixed[:, h * HD : (h + 1) * HD] = blended[i].astype(jnp.bfloat16)

        def project_peer(j):
            @pl.when(k == 0)
            def _():
                out_copy(1, j).wait()

            term = jnp.dot(mixed[...], wo_v[:, peer_cols(j)], preferred_element_type=jnp.float32)
            core_snd[k, :, half_cols(j)] = term.astype(jnp.bfloat16)
            sum_core(k, j).start()

        def project_own(j):
            @pl.when(k == 0)
            def _():
                out_copy(0, j).wait()

            part[:, half_cols(j)] = jnp.dot(
                mixed[...], wo_v[:, own_cols(j)], preferred_element_type=jnp.float32
            )

        def cross(j):
            sum_core(k, j).wait_recv()
            cols = half_cols(j)
            far = part[far_rows, cols] + core_rcv[k, far_rows, cols].astype(jnp.float32)
            tok_snd[k, :, cols] = far.astype(jnp.bfloat16)
            sum_tokens(k, j).start()
            memory = part[mem_rows, cols] + core_rcv[k, mem_rows, cols].astype(jnp.float32)
            mem_snd[k, :, cols] = memory.astype(jnp.bfloat16)
            sum_memory(k, j).start()
            part[mem_rows, cols] = memory + xin[k, mem_rows, own_cols(j)].astype(jnp.float32)
            part[own_rows, cols] = (
                part[own_rows, cols]
                + core_rcv[k, own_rows, cols].astype(jnp.float32)
                + xin[k, own_rows, own_cols(j)].astype(jnp.float32)
            )

        def finish_tokens(j):
            sum_tokens(k, j).wait_recv()
            cols = half_cols(j)
            state = part[own_rows, cols] + tok_rcv[k, :, cols].astype(jnp.float32)
            newt[k, :, own_cols(j)] = state.astype(jnp.bfloat16)

            @pl.when(has_next)
            def _():
                z_copy(k, j).start()

            out_tokens(k, j).start()

        def finish_memory(j):
            sum_memory(k, j).wait_recv()
            cols = half_cols(j)
            state = part[mem_rows, cols] + mem_rcv[k, :, cols].astype(jnp.float32)
            xin[k + 1, mem_rows, own_cols(j)] = state.astype(jnp.bfloat16)
            next_memory(k, j).start()

        project_peer(0)
        project_own(0)
        for j in range(1, CHUNKS):
            project_peer(j)
            project_own(j)
            cross(j - 1)
        cross(CHUNKS - 1)

        @pl.when(k > 0)
        def _():
            for j in range(CHUNKS):
                out_tokens(k - 1, j).wait_recv()
            emit_out(k - 1)

        for j in range(CHUNKS):
            finish_tokens(j)
            finish_memory(j)
        return carry

    lax.fori_loop(0, SEGS, segment, 0)
    for j in range(CHUNKS):
        out_tokens(SEGS - 1, j).wait_recv()
        next_memory(SEGS - 1, j).wait_recv()
    emit_out(SEGS - 1)

    def drain(k, carry):
        for j in range(CHUNKS):
            for copy in (
                sum_core(k, j), sum_tokens(k, j), sum_memory(k, j), next_memory(k, j),
                out_tokens(k, j),
            ):
                copy.wait_send()

            @pl.when(has_next)
            def _():
                z_copy(k, j).wait_send()

            @pl.when(has_prev)
            def _():
                for copy in (gather_x(k, j), gather_core(k, j), gather_far(k, j)):
                    copy.wait_send()

        return carry

    lax.fori_loop(0, SEGS, drain, 0)


def streamed(embeddings, lengths, mem_init, norm_gain, w_query, w_key, w_value, w_out):
    width = embeddings.shape[-1]
    q_cols, kv_cols = w_query.shape[1], w_key.shape[1]
    cosine, sine = rope_tables(HD)
    vmem = pl.BlockSpec(memory_space=pltpu.VMEM)
    anywhere = pl.BlockSpec(memory_space=pl.ANY)
    dma = pltpu.SemaphoreType.DMA
    half = jnp.bfloat16
    return pl.pallas_call(
        layer_kernel,
        out_shape=jax.ShapeDtypeStruct((1, SEGS, 32, width), half),
        in_specs=[pl.BlockSpec(memory_space=pltpu.SMEM)] + [vmem] * 3 + [anywhere] * 6,
        out_specs=vmem,
        scratch_shapes=[
            pltpu.VMEM((width, q_cols), half),
            pltpu.VMEM((width, kv_cols), half),
            pltpu.VMEM((width, kv_cols), half),
            pltpu.VMEM((q_cols, width), half),
            pltpu.VMEM((SEGS + 1, ROWS, width), half),
            pltpu.VMEM((SEGS, ROWS, width // 2), half),
            pltpu.VMEM((SEGS, ROWS, width // 2), half),
            pltpu.VMEM((SEGS, HALF_TOKENS, width // 2), half),
            pltpu.VMEM((SEGS, HALF_TOKENS, width // 2), half),
            pltpu.VMEM((SEGS, MEM, width // 2), half),
            pltpu.VMEM((SEGS, MEM, width // 2), half),
            pltpu.VMEM((SEGS, HALF_TOKENS, width), half),
            pltpu.VMEM((ROWS, width // 2), jnp.float32),
            pltpu.VMEM((ROWS, q_cols + 2 * kv_cols), jnp.float32),
            pltpu.VMEM((ROWS, q_cols), half),
            dma,
            dma((SEGS,)),
            dma((3, 2 * CHUNKS)),
            dma((2, CHUNKS)),
            dma((9, SEGS, CHUNKS)),
            dma((9, SEGS, CHUNKS)),
        ],
        compiler_params=pltpu.CompilerParams(
            collective_id=0, has_side_effects=True, vmem_limit_bytes=56 * 2**20
        ),
    )(
        lengths, norm_gain, jnp.asarray(cosine), jnp.asarray(sine), mem_init, embeddings,
        w_query, w_key, w_value, w_out,
    )


def solution(mesh):
    in_specs = (
        P("parts", None, None, None),
        P("parts", None),
        P(),
        P(),
        P(None, "tp"),
        P(None, "tp"),
        P(None, "tp"),
        P("tp", None),
    )
    out_specs = P("tp", "parts", None, None)
    body = streamed if mesh.shape["tp"] == SECTIONS * RANKS else local
    return jax.shard_map(body, mesh=mesh, in_specs=in_specs, out_specs=out_specs, check_vma=False)
```

```python
import jax
import jax.numpy as jnp
import numpy as np
from jax import lax
from jax.experimental import pallas as pl
from jax.experimental.pallas import tpu as pltpu
from jax.sharding import PartitionSpec as P

HD = 128
MEM = 32
SECTIONS = 4
SEGS = 3
SEG = 96


eps = 1e-05
rope_base = 500000.0


def from_partner(block, axis, bit):
    count = lax.axis_size(axis)
    route = []
    for low in range(count):
        high = low | 1 << bit
        if high != low and high < count:
            route += [(low, high), (high, low)]
    return lax.ppermute(block, axis, route)


def shortened(value):
    return jax.tree.map(lambda a: a.astype(jnp.bfloat16) if a.dtype == jnp.float32 else a, value)


def shifted(value, axis, by):
    peers = lax.axis_size(axis)
    pairs = [(i, i + by) for i in range(peers) if 0 <= i + by < peers]
    return lax.ppermute(value, axis, pairs)


def rotate(heads_in, positions):
    half_size = heads_in.shape[-1] // 2
    frequency = rope_base ** (
        -(jnp.arange(half_size, dtype=jnp.float32) * 2.0) / heads_in.shape[-1]
    )
    angles = positions.astype(jnp.float32)[:, None] * frequency[None, :]
    cosine = jnp.cos(angles)[:, None, :]
    sine_part = jnp.sin(angles)[:, None, :]
    first_half = heads_in[..., :half_size]
    second_half = heads_in[..., half_size:]
    return jnp.concatenate(
        [
            first_half * cosine - second_half * sine_part,
            second_half * cosine + first_half * sine_part,
        ],
        axis=-1,
    )


def visible(positions, length):
    query_ids = positions[:, None]
    key_ids = positions[None, :]
    real_key = (key_ids < MEM) | (key_ids - MEM < length)
    ordered = (key_ids <= query_ids) | (query_ids < MEM)
    return real_key & ordered


def normalize(widened, gain_row):
    scaled = widened * lax.rsqrt(jnp.mean(widened * widened, axis=-1, keepdims=True) + eps)
    return (scaled * gain_row).astype(jnp.bfloat16)


def attend(queries, key_heads, value_heads, positions, length):
    row_total = queries.shape[0]
    kv_local = key_heads.shape[1]
    grouped = queries.reshape(row_total, kv_local, -1, queries.shape[-1])
    scores = jnp.einsum(
        "qgrd,kgd->grqk", grouped, key_heads, preferred_element_type=jnp.float32
    ) * HD ** (-0.5)
    scores = jnp.where(visible(positions, length)[None, None], scores, -1e30)
    softmaxed = jax.nn.softmax(scores, axis=-1).astype(jnp.bfloat16)
    mixed = jnp.einsum(
        "grqk,kgd->qgrd", softmaxed, value_heads, preferred_element_type=jnp.float32
    ).astype(jnp.bfloat16)
    return mixed.reshape(row_total, -1)


def finish(widened, summed_out, length, row_ids):
    new_state = (widened + summed_out).astype(jnp.bfloat16)
    kept_rows = (row_ids < MEM) | (row_ids - MEM < length)
    return jnp.where(kept_rows[:, None], new_state, jnp.zeros_like(new_state))


def order_pair(mine, partner, lower_half):
    first_part = jnp.where(lower_half, mine, partner)
    second_part = jnp.where(lower_half, partner, mine)
    return jnp.concatenate([first_part, second_part], axis=0)


def gather_rows(piece, my_rank, seq_bits, rank_bits, level_list):
    stacked = piece
    for rank_bit in level_list:
        partner = from_partner(stacked, "tp", seq_bits + rank_bit)
        upper_half = my_rank // 2**rank_bit % 2 == 1
        stacked = jnp.where(
            upper_half, jnp.stack([partner, stacked], axis=0), jnp.stack([stacked, partner], axis=0)
        )
    axis_bits = list(reversed(level_list))
    order_axes = [axis_bits.index(rank_bit) for rank_bit in reversed(range(rank_bits))]
    stacked = jnp.transpose(stacked, order_axes + [rank_bits, rank_bits + 1])
    return stacked.reshape(2**rank_bits * piece.shape[0], piece.shape[-1])


def scatter_rows(partial_term, my_rank, seq_bits, rank_bits, level_list, shard_rows):
    model_width = partial_term.shape[-1]
    running = partial_term.reshape((2,) * rank_bits + (shard_rows, model_width))
    axis_bits = list(reversed(range(rank_bits)))
    for rank_bit in level_list:
        position = axis_bits.index(rank_bit)
        upper_half = my_rank // 2**rank_bit % 2 == 1
        low_part = lax.index_in_dim(running, 0, position, keepdims=False)
        high_part = lax.index_in_dim(running, 1, position, keepdims=False)
        kept_rows = jnp.where(upper_half, high_part, low_part)
        sent_rows = jnp.where(upper_half, low_part, high_part)
        running = kept_rows + from_partner(
            sent_rows.astype(jnp.bfloat16), "tp", seq_bits + rank_bit
        ).astype(sent_rows.dtype)
        axis_bits = [other_bit for other_bit in axis_bits if other_bit != rank_bit]
    return running


def local(embeddings, lengths, mem_init, norm_gain, w_query, w_key, w_value, w_out):
    axis_width = lax.axis_size("tp")
    group_size = axis_width // SECTIONS
    rank_count = min(8, group_size)
    seq_count = group_size // rank_count
    seq_bits = seq_count.bit_length() - 1
    rank_bits = rank_count.bit_length() - 1
    device_index = lax.axis_index("tp")
    group_index = device_index // group_size
    my_rank = device_index % group_size // seq_count
    my_seq = device_index % seq_count
    model_width = embeddings.shape[-1]
    row_total = SEG + MEM
    shard_rows = row_total // rank_count
    mem_block = MEM // rank_count
    token_block = SEG // rank_count
    within = jnp.arange(shard_rows, dtype=jnp.int32)
    block_ids = jnp.arange(rank_count, dtype=jnp.int32)[:, None]
    positions = jnp.where(
        within[None, :] < mem_block,
        block_ids * mem_block + within[None, :],
        MEM + block_ids * token_block + within[None, :] - mem_block,
    ).reshape(-1)
    row_ids = lax.dynamic_index_in_dim(
        positions.reshape(rank_count, shard_rows), my_rank, 0, keepdims=False
    )
    gain_row = lax.dynamic_index_in_dim(norm_gain, group_index, 0, keepdims=False)
    my_lengths = lax.dynamic_index_in_dim(lengths, my_seq, 0, keepdims=False)
    first_memory = lax.dynamic_slice(
        mem_init, (group_index, my_rank * mem_block, 0), (1, mem_block, model_width)
    ).reshape(mem_block, model_width)
    query_stack, key_stack, value_stack, out_stack = (
        w_query[None],
        w_key[None],
        w_value[None],
        w_out[None],
    )
    for seq_bit in range(seq_bits):
        partner_query, partner_key, partner_value, partner_out = (
            from_partner(shortened(query_stack), "tp", seq_bit).astype(query_stack.dtype),
            from_partner(shortened(key_stack), "tp", seq_bit).astype(key_stack.dtype),
            from_partner(shortened(value_stack), "tp", seq_bit).astype(value_stack.dtype),
            from_partner(shortened(out_stack), "tp", seq_bit).astype(out_stack.dtype),
        )
        lower_half = device_index // 2**seq_bit % 2 == 0
        query_stack = order_pair(query_stack, partner_query, lower_half)
        key_stack = order_pair(key_stack, partner_key, lower_half)
        value_stack = order_pair(value_stack, partner_value, lower_half)
        out_stack = order_pair(out_stack, partner_out, lower_half)
    level_list = list(range(rank_bits))
    states = jnp.zeros((SEGS, shard_rows, model_width), jnp.bfloat16)
    memory = jnp.zeros((mem_block, model_width), jnp.bfloat16)
    arrived = jnp.zeros((token_block, model_width), jnp.bfloat16)
    step_total = SEGS + SECTIONS - 1
    for step_index in range(step_total):
        segment = step_index - group_index
        active = (segment >= 0) & (segment < SEGS)
        clipped = jnp.clip(segment, 0, SEGS - 1)
        length = lax.dynamic_index_in_dim(my_lengths, clipped, 0, keepdims=False)
        embedded = lax.dynamic_slice(
            embeddings,
            (my_seq, clipped, my_rank * token_block, 0),
            (1, 1, token_block, model_width),
        ).reshape(token_block, model_width)
        token_source = jnp.where(group_index == 0, embedded, arrived)
        memory_source = jnp.where(segment == 0, first_memory, memory)
        inputs = jnp.concatenate([memory_source, token_source], axis=0)
        widened = inputs.astype(jnp.float32)
        normed = normalize(widened, gain_row)
        gathered = gather_rows(normed, my_rank, seq_bits, rank_bits, level_list)
        query_all = jnp.einsum(
            "rd,sdc->rsc", gathered, query_stack, preferred_element_type=jnp.float32
        )
        queries = rotate(query_all.reshape(row_total, -1, HD), positions).astype(jnp.bfloat16)
        key_all = jnp.einsum("rd,sdc->rsc", gathered, key_stack, preferred_element_type=jnp.float32)
        key_raw = lax.optimization_barrier(key_all.reshape(row_total, -1).astype(jnp.bfloat16))
        value_all = jnp.einsum(
            "rd,sdc->rsc", gathered, value_stack, preferred_element_type=jnp.float32
        ).astype(jnp.bfloat16)
        key_heads = rotate(
            key_raw.astype(jnp.float32).reshape(row_total, -1, HD), positions
        ).astype(jnp.bfloat16)
        value_heads = value_all.reshape(row_total, -1, HD)
        mixed_heads = attend(queries, key_heads, value_heads, positions, length)
        mixed_split = mixed_heads.reshape(row_total, out_stack.shape[0], out_stack.shape[1])
        partial_term = jnp.einsum(
            "rsc,scd->rd", mixed_split, out_stack, preferred_element_type=jnp.float32
        )
        summed_out = scatter_rows(
            partial_term, my_rank, seq_bits, rank_bits, level_list, shard_rows
        )
        new_state = finish(widened, summed_out, length, row_ids)
        memory = jnp.where(active, new_state[:mem_block], memory)
        states = jnp.where(
            active, lax.dynamic_update_index_in_dim(states, new_state, clipped, 0), states
        )
        if step_index + 1 < step_total:
            arrived = shifted(new_state[mem_block:], "tp", group_size)
    return states[None]


RANKS = 4
WIDTHS = (512, 512, 512, 512)
STARTS = tuple(sum(WIDTHS[:j]) for j in range(len(WIDTHS)))
CHUNKS = len(WIDTHS)
ROWS = SEG + MEM
GATHER = "x0 g0 x1 g1 h0 x2 g2 h1 x3 g3 h2 h3".split()
FINISH = "p0 o0 p1 o1 c0 p2 o2 c1 p3 o3 c2:4 m0:4 e0 t0:4 z0:4 f0:4".split()


def span(step):
    low, high = step[1:].split(":") if ":" in step else (step[1:], int(step[1:]) + 1)
    return int(low), int(high)


HALF_TOKENS = SEG // 2
MESH = pl.DeviceIdType.MESH


def rope_tables(head):
    half = head // 2
    frequency = rope_base ** (-(np.arange(half, dtype=np.float64) * 2.0) / head)
    angles = np.arange(ROWS)[:, None] * frequency[None, :]
    cosine, sine = np.cos(angles), np.sin(angles)
    return (
        np.concatenate([cosine, cosine], axis=1).astype(np.float32),
        np.concatenate([-sine, sine], axis=1).astype(np.float32),
    )


def layer_kernel(
    len_ref, gain_ref, cos_ref, sin_ref, m0_ref, emb_ref, wq_ref, wk_ref, wv_ref, wo_ref,
    out_ref,
    wq_v, wk_v, wv_v, wo_v, xin, core_snd, core_rcv, tok_snd, tok_rcv, mem_snd, mem_rcv, newt,
    part, acc, mixed, gain_v, cos_v, sin_v, out_v,
    msem, esem, wsem, osem, ssem, fsem, send_sem, recv_sem,
):
    width = xin.shape[-1]
    half = width // 2
    q_cols, kv_cols = wq_v.shape[1], wk_v.shape[1]
    me = lax.axis_index("tp")
    group, rank = me // RANKS, me % RANKS
    xb, cb = rank // 2, rank % 2
    core_peer = group * RANKS + xb * 2 + (1 - cb)
    x_peer = group * RANKS + (1 - xb) * 2 + (1 - cb)
    has_next, has_prev = group < SECTIONS - 1, group > 0
    next_peer, prev_peer = me + RANKS, me - RANKS
    side = (rank // 2 + rank % 2) % 2
    own_rows = pl.ds(pl.multiple_of(MEM + xb * HALF_TOKENS, 16), HALF_TOKENS)
    far_rows = pl.ds(pl.multiple_of(MEM + (1 - xb) * HALF_TOKENS, 16), HALF_TOKENS)
    mem_rows = pl.ds(0, MEM)

    def reach(low, high=None):
        return STARTS[low], sum(WIDTHS[low : low + 1 if high is None else high])

    def own_cols(low, high=None):
        start, size = reach(low, high)
        return pl.ds(pl.multiple_of(side * half + start, 128), size)

    def peer_cols(low, high=None):
        start, size = reach(low, high)
        return pl.ds(pl.multiple_of((1 - side) * half + start, 128), size)

    def half_cols(low, high=None):
        return pl.ds(*reach(low, high))

    blocks_in = [(step[0] == "g", *span(step)) for step in GATHER if step[0] in "gh"]
    blocks_out = [(step[0] == "o", *span(step)) for step in FINISH if step[0] in "po"]
    peer_out = {low: high for mine, low, high in blocks_out if not mine}

    def block_cols(mine, low, high):
        return own_cols(low, high) if mine else peer_cols(low, high)

    def weight_copies(o):
        cols = block_cols(*blocks_in[o])
        return [
            pltpu.make_async_copy(src.at[cols], dst.at[cols], wsem.at[i, o])
            for i, (src, dst) in enumerate(((wq_ref, wq_v), (wk_ref, wk_v), (wv_ref, wv_v)))
        ]

    def out_copy(o):
        cols = block_cols(*blocks_out[o])
        return pltpu.make_async_copy(wo_ref.at[:, cols], wo_v.at[:, cols], osem.at[o])

    def in_copy(k):
        return pltpu.make_async_copy(
            emb_ref.at[0, k], xin.at[k, pl.ds(MEM, SEG)], esem.at[k]
        )

    def remote(src, dst, kind, k, j, peer):
        return pltpu.make_async_remote_copy(
            src_ref=src, dst_ref=dst, send_sem=send_sem.at[kind, k, j],
            recv_sem=recv_sem.at[kind, k, j],
            device_id={"tp": peer}, device_id_type=MESH,
        )

    def in_place(ref, kind, k, j, peer):
        return remote(ref, ref, kind, k, j, peer)

    def z_copy(k, j):
        return remote(
            newt.at[k, :, own_cols(j)], xin.at[k, own_rows, own_cols(j)], 0, k, j, next_peer
        )

    def gather_x(k, j):
        return in_place(xin.at[k, own_rows, own_cols(j)], 1, k, j, x_peer)

    def gather_core(k, j):
        return in_place(xin.at[k, own_rows, own_cols(j)], 2, k, j, core_peer)

    def gather_far(k, j):
        return in_place(xin.at[k, far_rows, own_cols(j)], 3, k, j, core_peer)

    def sum_core(k, low):
        cols = half_cols(low, peer_out[low])
        return remote(core_snd.at[k, :, cols], core_rcv.at[k, :, cols], 4, k, low, core_peer)

    def sum_tokens(k, j):
        return remote(
            tok_snd.at[k, :, half_cols(j)], tok_rcv.at[k, :, half_cols(j)], 5, k, j, x_peer
        )

    def sum_memory(k, j):
        return remote(
            mem_snd.at[k, :, half_cols(j)], mem_rcv.at[k, :, half_cols(j)], 6, k, j, x_peer
        )

    def next_memory(k, j):
        return in_place(xin.at[k + 1, mem_rows, own_cols(j)], 7, k, j, core_peer)

    def out_tokens(k, j):
        return in_place(newt.at[k, :, own_cols(j)], 8, k, j, core_peer)

    first_memory = pltpu.make_async_copy(m0_ref.at[group], xin.at[0, mem_rows], msem)
    gain_copy = pltpu.make_async_copy(gain_ref, gain_v, ssem.at[0])
    cos_copy = pltpu.make_async_copy(cos_ref, cos_v, ssem.at[1])
    sin_copy = pltpu.make_async_copy(sin_ref, sin_v, ssem.at[2])

    def start_weights(o):
        for copy in weight_copies(o):
            copy.start()

    def out_block(k):
        return pltpu.make_async_copy(out_v.at[k], out_ref.at[0, k], fsem.at[k])

    @pl.when(group == 0)
    def _():
        in_copy(0).start()

    first_memory.start()
    gain_copy.start()
    start_weights(0)
    start_weights(1)

    barrier = pltpu.get_barrier_semaphore()
    for peer in (core_peer, x_peer):
        pl.semaphore_signal(barrier, inc=1, device_id={"tp": peer}, device_id_type=MESH)

    @pl.when(has_next)
    def _():
        pl.semaphore_signal(barrier, inc=1, device_id={"tp": next_peer}, device_id_type=MESH)

    @pl.when(has_prev)
    def _():
        pl.semaphore_signal(barrier, inc=1, device_id={"tp": prev_peer}, device_id_type=MESH)

    for o in range(2, len(blocks_in)):
        start_weights(o)
    cos_copy.start()
    sin_copy.start()
    for o in range(len(blocks_out)):
        out_copy(o).start()

    @pl.when(group == 0)
    def _():
        for k in range(1, SEGS):
            in_copy(k).start()

    inner = has_next & has_prev

    @pl.when(inner)
    def _():
        pl.semaphore_wait(barrier, 4)

    @pl.when(has_prev & jnp.logical_not(has_next))
    def _():
        pl.semaphore_wait(barrier, 3)

    first_memory.wait()
    gain_copy.wait()

    def pass_on(k, j):
        @pl.when(has_prev)
        def _():
            z_copy(k, j).wait_recv()
            gather_x(k, j).start()
            gather_core(k, j).start()

    def pass_far(k, j):
        @pl.when(has_prev)
        def _():
            gather_x(k, j).wait_recv()
            gather_far(k, j).start()

    def rope(block):
        return block * cos_v[...] + pltpu.roll(block, HD // 2, 1) * sin_v[...]

    def emit_out(k):
        length = len_ref[0, k]
        step = half // 4
        row = lax.broadcasted_iota(jnp.int32, (32, step), 0)
        kept = (row < 8) | (xb * HALF_TOKENS + cb * 24 + row - 8 < length)
        for j in range(8):
            cols = pl.ds(j * step, step)
            memory = xin[k + 1, mem_rows, cols].astype(jnp.float32)
            tokens = newt[k, :, cols].astype(jnp.float32)
            low = jnp.where(xb == 0, memory[:16], memory[16:])
            block = jnp.concatenate(
                [
                    jnp.where(cb == 0, low[:8], low[8:]),
                    jnp.where(cb == 0, tokens[:24], tokens[24:]),
                ],
                axis=0,
            )
            out_v[k, :, cols] = jnp.where(kept, block, 0.0).astype(jnp.bfloat16)
        out_block(k).start()

    def segment(k, carry):
        length = len_ref[0, k]
        squares = jnp.zeros((ROWS, 1), jnp.float32)

        @pl.when(group == 0)
        def _():
            in_copy(k).wait()

        o = 0
        for step in GATHER:
            kind, (j, last) = step[0], span(step)
            if kind == "z":
                pass_on(k, j)
                continue
            if kind == "x":
                pass_far(k, j)
                continue
            if kind == "h":

                @pl.when(has_prev)
                def _():
                    for i in range(j, last):
                        gather_core(k, i).wait_recv()
                        gather_far(k, i).wait_recv()

                @pl.when(k > 0)
                def _():
                    for i in range(j, last):
                        next_memory(k - 1, i).wait_recv()

            @pl.when(k == 0)
            def _():
                for copy in weight_copies(o):
                    copy.wait()

            cols = block_cols(*blocks_in[o])
            raw = xin[k, :, cols].astype(jnp.float32)
            squares = squares + jnp.sum(raw * raw, axis=1, keepdims=True)
            gained = (raw * gain_v[pl.ds(group, 1), cols]).astype(jnp.bfloat16)
            low = 0
            for weight in (wq_v, wk_v, wv_v):
                high = low + weight.shape[1]
                term = jnp.dot(gained, weight[cols], preferred_element_type=jnp.float32)
                if o == 0:
                    acc[:, low:high] = term
                else:
                    acc[:, low:high] += term
                low = high
            o += 1

        @pl.when(k == 0)
        def _():
            cos_copy.wait()
            sin_copy.wait()

        @pl.when((k == 0) & (group == 0))
        def _():
            pl.semaphore_wait(barrier, 3)

        factor = lax.rsqrt(squares * (1.0 / width) + eps)
        query_pos = lax.broadcasted_iota(jnp.int32, (ROWS, ROWS), 0)
        key_pos = lax.broadcasted_iota(jnp.int32, (ROWS, ROWS), 1)
        real_key = (key_pos < MEM) | (key_pos - MEM < length)
        ordered = (key_pos <= query_pos) | (query_pos < MEM)
        bias = jnp.where(real_key & ordered, 0.0, -1e30).astype(jnp.float32)
        per_kv = q_cols // kv_cols
        for g in range(kv_cols // HD):
            key_raw = (acc[:, q_cols + g * HD : q_cols + (g + 1) * HD] * factor).astype(
                jnp.bfloat16
            )
            key = rope(key_raw.astype(jnp.float32)).astype(jnp.bfloat16)
            low = q_cols + kv_cols + g * HD
            value = (acc[:, low : low + HD] * factor).astype(jnp.bfloat16)
            heads = range(g * per_kv, (g + 1) * per_kv)
            queries = jnp.concatenate(
                [
                    rope(acc[:, h * HD : (h + 1) * HD] * factor).astype(jnp.bfloat16)
                    for h in heads
                ],
                axis=0,
            )
            scores = lax.dot_general(
                queries, key, (((1,), (1,)), ((), ())), preferred_element_type=jnp.float32
            ) * HD ** (-0.5)
            scores = scores.reshape(per_kv, ROWS, ROWS) + bias[None]
            weight = jnp.exp(scores - jnp.max(scores, axis=2, keepdims=True))
            share = 1.0 / jnp.sum(weight, axis=2, keepdims=True)
            blended = jnp.dot(
                weight.astype(jnp.bfloat16).reshape(per_kv * ROWS, ROWS),
                value,
                preferred_element_type=jnp.float32,
            ).reshape(per_kv, ROWS, HD) * share
            for i, h in enumerate(heads):
                mixed[:, h * HD : (h + 1) * HD] = blended[i].astype(jnp.bfloat16)

        def project_peer(low, high):
            @pl.when(k == 0)
            def _():
                out_copy(blocks_out.index((False, low, high))).wait()

            term = jnp.dot(
                mixed[...], wo_v[:, peer_cols(low, high)], preferred_element_type=jnp.float32
            )
            core_snd[k, :, half_cols(low, high)] = term.astype(jnp.bfloat16)
            sum_core(k, low).start()

        def project_own(low, high):
            @pl.when(k == 0)
            def _():
                out_copy(blocks_out.index((True, low, high))).wait()

            part[:, half_cols(low, high)] = jnp.dot(
                mixed[...], wo_v[:, own_cols(low, high)], preferred_element_type=jnp.float32
            )

        def cross(j):
            if j in peer_out:
                sum_core(k, j).wait_recv()
            cols = half_cols(j)
            far = part[far_rows, cols] + core_rcv[k, far_rows, cols].astype(jnp.float32)
            tok_snd[k, :, cols] = far.astype(jnp.bfloat16)
            sum_tokens(k, j).start()
            part[own_rows, cols] = (
                part[own_rows, cols]
                + core_rcv[k, own_rows, cols].astype(jnp.float32)
                + xin[k, own_rows, own_cols(j)].astype(jnp.float32)
            )

        def cross_memory(j):
            cols = half_cols(j)
            memory = part[mem_rows, cols] + core_rcv[k, mem_rows, cols].astype(jnp.float32)
            mem_snd[k, :, cols] = memory.astype(jnp.bfloat16)
            sum_memory(k, j).start()
            part[mem_rows, cols] = memory + xin[k, mem_rows, own_cols(j)].astype(jnp.float32)

        def finish_tokens(j):
            sum_tokens(k, j).wait_recv()
            cols = half_cols(j)
            state = part[own_rows, cols] + tok_rcv[k, :, cols].astype(jnp.float32)
            newt[k, :, own_cols(j)] = state.astype(jnp.bfloat16)

            @pl.when(has_next)
            def _():
                z_copy(k, j).start()

            out_tokens(k, j).start()

        def finish_memory(j):
            sum_memory(k, j).wait_recv()
            cols = half_cols(j)
            state = part[mem_rows, cols] + mem_rcv[k, :, cols].astype(jnp.float32)
            xin[k + 1, mem_rows, own_cols(j)] = state.astype(jnp.bfloat16)
            next_memory(k, j).start()

        def emit_last(j):
            @pl.when(k > 0)
            def _():
                for i in range(CHUNKS):
                    out_tokens(k - 1, i).wait_recv()
                emit_out(k - 1)

        def pass_next(j):
            @pl.when(k + 1 < SEGS)
            def _():
                pass_on(k + 1, j)

        def pass_far_next(j):
            @pl.when(k + 1 < SEGS)
            def _():
                pass_far(k + 1, j)

        actions = {
            "p": project_peer, "o": project_own, "c": cross, "m": cross_memory,
            "t": finish_tokens, "f": finish_memory, "e": emit_last, "z": pass_next,
            "x": pass_far_next,
        }
        for step in FINISH:
            if step[0] in "po":
                actions[step[0]](*span(step))
            else:
                for j in range(*span(step)):
                    actions[step[0]](j)
        return carry

    for j in range(CHUNKS):
        pass_on(0, j)
    lax.fori_loop(0, SEGS, segment, 0)
    for j in range(CHUNKS):
        out_tokens(SEGS - 1, j).wait_recv()
        next_memory(SEGS - 1, j).wait_recv()
    emit_out(SEGS - 1)

    def drain(k, carry):
        for low in peer_out:
            sum_core(k, low).wait_send()
        for j in range(CHUNKS):
            for copy in (
                sum_tokens(k, j), sum_memory(k, j), next_memory(k, j),
                out_tokens(k, j),
            ):
                copy.wait_send()

            @pl.when(has_next)
            def _():
                z_copy(k, j).wait_send()

            @pl.when(has_prev)
            def _():
                gather_x(k, j).wait_send()
                gather_core(k, j).wait_send()
                gather_far(k, j).wait_send()


        return carry

    lax.fori_loop(0, SEGS, drain, 0)
    for k in range(SEGS):
        out_block(k).wait()


def streamed(embeddings, lengths, mem_init, norm_gain, w_query, w_key, w_value, w_out):
    width = embeddings.shape[-1]
    q_cols, kv_cols = w_query.shape[1], w_key.shape[1]
    cosine, sine = rope_tables(HD)
    anywhere = pl.BlockSpec(memory_space=pl.ANY)
    dma = pltpu.SemaphoreType.DMA
    half = jnp.bfloat16
    return pl.pallas_call(
        layer_kernel,
        out_shape=jax.ShapeDtypeStruct((1, SEGS, 32, width), half),
        in_specs=[pl.BlockSpec(memory_space=pltpu.SMEM)] + [anywhere] * 9,
        out_specs=anywhere,
        scratch_shapes=[
            pltpu.VMEM((width, q_cols), half),
            pltpu.VMEM((width, kv_cols), half),
            pltpu.VMEM((width, kv_cols), half),
            pltpu.VMEM((q_cols, width), half),
            pltpu.VMEM((SEGS + 1, ROWS, width), half),
            pltpu.VMEM((SEGS, ROWS, width // 2), half),
            pltpu.VMEM((SEGS, ROWS, width // 2), half),
            pltpu.VMEM((SEGS, HALF_TOKENS, width // 2), half),
            pltpu.VMEM((SEGS, HALF_TOKENS, width // 2), half),
            pltpu.VMEM((SEGS, MEM, width // 2), half),
            pltpu.VMEM((SEGS, MEM, width // 2), half),
            pltpu.VMEM((SEGS, HALF_TOKENS, width), half),
            pltpu.VMEM((ROWS, width // 2), jnp.float32),
            pltpu.VMEM((ROWS, q_cols + 2 * kv_cols), jnp.float32),
            pltpu.VMEM((ROWS, q_cols), half),
            pltpu.VMEM(norm_gain.shape, jnp.float32),
            pltpu.VMEM((ROWS, HD), jnp.float32),
            pltpu.VMEM((ROWS, HD), jnp.float32),
            pltpu.VMEM((SEGS, 32, width), half),
            dma,
            dma((SEGS,)),
            dma((3, 2 * CHUNKS)),
            dma((2 * CHUNKS,)),
            dma((3,)),
            dma((SEGS,)),
            dma((9, SEGS, CHUNKS)),
            dma((9, SEGS, CHUNKS)),
        ],
        compiler_params=pltpu.CompilerParams(
            collective_id=0, has_side_effects=True, vmem_limit_bytes=56 * 2**20
        ),
    )(
        lengths, norm_gain, jnp.asarray(cosine), jnp.asarray(sine), mem_init, embeddings,
        w_query, w_key, w_value, w_out,
    )


def solution(mesh):
    in_specs = (
        P("parts", None, None, None),
        P("parts", None),
        P(),
        P(),
        P(None, "tp"),
        P(None, "tp"),
        P(None, "tp"),
        P("tp", None),
    )
    out_specs = P("tp", "parts", None, None)
    body = streamed if mesh.shape["tp"] == SECTIONS * RANKS else local
    return jax.shard_map(body, mesh=mesh, in_specs=in_specs, out_specs=out_specs, check_vma=False)
```

```python
import jax
import jax.numpy as jnp
import numpy as np
from jax import lax
from jax.experimental import pallas as pl
from jax.experimental.pallas import tpu as pltpu
from jax.sharding import PartitionSpec as P

HD = 128
MEM = 32
SECTIONS = 4
SEGS = 3
SEG = 96


eps = 1e-05
rope_base = 500000.0


def from_partner(block, axis, bit):
    count = lax.axis_size(axis)
    route = []
    for low in range(count):
        high = low | 1 << bit
        if high != low and high < count:
            route += [(low, high), (high, low)]
    return lax.ppermute(block, axis, route)


def shortened(value):
    return jax.tree.map(lambda a: a.astype(jnp.bfloat16) if a.dtype == jnp.float32 else a, value)


def shifted(value, axis, by):
    peers = lax.axis_size(axis)
    pairs = [(i, i + by) for i in range(peers) if 0 <= i + by < peers]
    return lax.ppermute(value, axis, pairs)


def rotate(heads_in, positions):
    half_size = heads_in.shape[-1] // 2
    frequency = rope_base ** (
        -(jnp.arange(half_size, dtype=jnp.float32) * 2.0) / heads_in.shape[-1]
    )
    angles = positions.astype(jnp.float32)[:, None] * frequency[None, :]
    cosine = jnp.cos(angles)[:, None, :]
    sine_part = jnp.sin(angles)[:, None, :]
    first_half = heads_in[..., :half_size]
    second_half = heads_in[..., half_size:]
    return jnp.concatenate(
        [
            first_half * cosine - second_half * sine_part,
            second_half * cosine + first_half * sine_part,
        ],
        axis=-1,
    )


def visible(positions, length):
    query_ids = positions[:, None]
    key_ids = positions[None, :]
    real_key = (key_ids < MEM) | (key_ids - MEM < length)
    ordered = (key_ids <= query_ids) | (query_ids < MEM)
    return real_key & ordered


def normalize(widened, gain_row):
    scaled = widened * lax.rsqrt(jnp.mean(widened * widened, axis=-1, keepdims=True) + eps)
    return (scaled * gain_row).astype(jnp.bfloat16)


def attend(queries, key_heads, value_heads, positions, length):
    row_total = queries.shape[0]
    kv_local = key_heads.shape[1]
    grouped = queries.reshape(row_total, kv_local, -1, queries.shape[-1])
    scores = jnp.einsum(
        "qgrd,kgd->grqk", grouped, key_heads, preferred_element_type=jnp.float32
    ) * HD ** (-0.5)
    scores = jnp.where(visible(positions, length)[None, None], scores, -1e30)
    softmaxed = jax.nn.softmax(scores, axis=-1).astype(jnp.bfloat16)
    mixed = jnp.einsum(
        "grqk,kgd->qgrd", softmaxed, value_heads, preferred_element_type=jnp.float32
    ).astype(jnp.bfloat16)
    return mixed.reshape(row_total, -1)


def finish(widened, summed_out, length, row_ids):
    new_state = (widened + summed_out).astype(jnp.bfloat16)
    kept_rows = (row_ids < MEM) | (row_ids - MEM < length)
    return jnp.where(kept_rows[:, None], new_state, jnp.zeros_like(new_state))


def order_pair(mine, partner, lower_half):
    first_part = jnp.where(lower_half, mine, partner)
    second_part = jnp.where(lower_half, partner, mine)
    return jnp.concatenate([first_part, second_part], axis=0)


def gather_rows(piece, my_rank, seq_bits, rank_bits, level_list):
    stacked = piece
    for rank_bit in level_list:
        partner = from_partner(stacked, "tp", seq_bits + rank_bit)
        upper_half = my_rank // 2**rank_bit % 2 == 1
        stacked = jnp.where(
            upper_half, jnp.stack([partner, stacked], axis=0), jnp.stack([stacked, partner], axis=0)
        )
    axis_bits = list(reversed(level_list))
    order_axes = [axis_bits.index(rank_bit) for rank_bit in reversed(range(rank_bits))]
    stacked = jnp.transpose(stacked, order_axes + [rank_bits, rank_bits + 1])
    return stacked.reshape(2**rank_bits * piece.shape[0], piece.shape[-1])


def scatter_rows(partial_term, my_rank, seq_bits, rank_bits, level_list, shard_rows):
    model_width = partial_term.shape[-1]
    running = partial_term.reshape((2,) * rank_bits + (shard_rows, model_width))
    axis_bits = list(reversed(range(rank_bits)))
    for rank_bit in level_list:
        position = axis_bits.index(rank_bit)
        upper_half = my_rank // 2**rank_bit % 2 == 1
        low_part = lax.index_in_dim(running, 0, position, keepdims=False)
        high_part = lax.index_in_dim(running, 1, position, keepdims=False)
        kept_rows = jnp.where(upper_half, high_part, low_part)
        sent_rows = jnp.where(upper_half, low_part, high_part)
        running = kept_rows + from_partner(
            sent_rows.astype(jnp.bfloat16), "tp", seq_bits + rank_bit
        ).astype(sent_rows.dtype)
        axis_bits = [other_bit for other_bit in axis_bits if other_bit != rank_bit]
    return running


def local(embeddings, lengths, mem_init, norm_gain, w_query, w_key, w_value, w_out):
    axis_width = lax.axis_size("tp")
    group_size = axis_width // SECTIONS
    rank_count = min(8, group_size)
    seq_count = group_size // rank_count
    seq_bits = seq_count.bit_length() - 1
    rank_bits = rank_count.bit_length() - 1
    device_index = lax.axis_index("tp")
    group_index = device_index // group_size
    my_rank = device_index % group_size // seq_count
    my_seq = device_index % seq_count
    model_width = embeddings.shape[-1]
    row_total = SEG + MEM
    shard_rows = row_total // rank_count
    mem_block = MEM // rank_count
    token_block = SEG // rank_count
    within = jnp.arange(shard_rows, dtype=jnp.int32)
    block_ids = jnp.arange(rank_count, dtype=jnp.int32)[:, None]
    positions = jnp.where(
        within[None, :] < mem_block,
        block_ids * mem_block + within[None, :],
        MEM + block_ids * token_block + within[None, :] - mem_block,
    ).reshape(-1)
    row_ids = lax.dynamic_index_in_dim(
        positions.reshape(rank_count, shard_rows), my_rank, 0, keepdims=False
    )
    gain_row = lax.dynamic_index_in_dim(norm_gain, group_index, 0, keepdims=False)
    my_lengths = lax.dynamic_index_in_dim(lengths, my_seq, 0, keepdims=False)
    first_memory = lax.dynamic_slice(
        mem_init, (group_index, my_rank * mem_block, 0), (1, mem_block, model_width)
    ).reshape(mem_block, model_width)
    query_stack, key_stack, value_stack, out_stack = (
        w_query[None],
        w_key[None],
        w_value[None],
        w_out[None],
    )
    for seq_bit in range(seq_bits):
        partner_query, partner_key, partner_value, partner_out = (
            from_partner(shortened(query_stack), "tp", seq_bit).astype(query_stack.dtype),
            from_partner(shortened(key_stack), "tp", seq_bit).astype(key_stack.dtype),
            from_partner(shortened(value_stack), "tp", seq_bit).astype(value_stack.dtype),
            from_partner(shortened(out_stack), "tp", seq_bit).astype(out_stack.dtype),
        )
        lower_half = device_index // 2**seq_bit % 2 == 0
        query_stack = order_pair(query_stack, partner_query, lower_half)
        key_stack = order_pair(key_stack, partner_key, lower_half)
        value_stack = order_pair(value_stack, partner_value, lower_half)
        out_stack = order_pair(out_stack, partner_out, lower_half)
    level_list = list(range(rank_bits))
    states = jnp.zeros((SEGS, shard_rows, model_width), jnp.bfloat16)
    memory = jnp.zeros((mem_block, model_width), jnp.bfloat16)
    arrived = jnp.zeros((token_block, model_width), jnp.bfloat16)
    step_total = SEGS + SECTIONS - 1
    for step_index in range(step_total):
        segment = step_index - group_index
        active = (segment >= 0) & (segment < SEGS)
        clipped = jnp.clip(segment, 0, SEGS - 1)
        length = lax.dynamic_index_in_dim(my_lengths, clipped, 0, keepdims=False)
        embedded = lax.dynamic_slice(
            embeddings,
            (my_seq, clipped, my_rank * token_block, 0),
            (1, 1, token_block, model_width),
        ).reshape(token_block, model_width)
        token_source = jnp.where(group_index == 0, embedded, arrived)
        memory_source = jnp.where(segment == 0, first_memory, memory)
        inputs = jnp.concatenate([memory_source, token_source], axis=0)
        widened = inputs.astype(jnp.float32)
        normed = normalize(widened, gain_row)
        gathered = gather_rows(normed, my_rank, seq_bits, rank_bits, level_list)
        query_all = jnp.einsum(
            "rd,sdc->rsc", gathered, query_stack, preferred_element_type=jnp.float32
        )
        queries = rotate(query_all.reshape(row_total, -1, HD), positions).astype(jnp.bfloat16)
        key_all = jnp.einsum("rd,sdc->rsc", gathered, key_stack, preferred_element_type=jnp.float32)
        key_raw = lax.optimization_barrier(key_all.reshape(row_total, -1).astype(jnp.bfloat16))
        value_all = jnp.einsum(
            "rd,sdc->rsc", gathered, value_stack, preferred_element_type=jnp.float32
        ).astype(jnp.bfloat16)
        key_heads = rotate(
            key_raw.astype(jnp.float32).reshape(row_total, -1, HD), positions
        ).astype(jnp.bfloat16)
        value_heads = value_all.reshape(row_total, -1, HD)
        mixed_heads = attend(queries, key_heads, value_heads, positions, length)
        mixed_split = mixed_heads.reshape(row_total, out_stack.shape[0], out_stack.shape[1])
        partial_term = jnp.einsum(
            "rsc,scd->rd", mixed_split, out_stack, preferred_element_type=jnp.float32
        )
        summed_out = scatter_rows(
            partial_term, my_rank, seq_bits, rank_bits, level_list, shard_rows
        )
        new_state = finish(widened, summed_out, length, row_ids)
        memory = jnp.where(active, new_state[:mem_block], memory)
        states = jnp.where(
            active, lax.dynamic_update_index_in_dim(states, new_state, clipped, 0), states
        )
        if step_index + 1 < step_total:
            arrived = shifted(new_state[mem_block:], "tp", group_size)
    return states[None]


RANKS = 4
WIDTHS = (512, 512, 512, 512)
STARTS = tuple(sum(WIDTHS[:j]) for j in range(len(WIDTHS)))
CHUNKS = len(WIDTHS)
ROWS = SEG + MEM
GATHER = ('x0', 'g0', 'x1', 'g1', 'h0', 'x2', 'g2', 'h1', 'x3', 'g3', 'h2', 'h3')
FINISH = ('p0', 'o0', 'p1', 'o1', 'c0', 'p2', 'o2', 'c1', 'p3', 'o3', 'c2:4', 'm0:2', 'm2:4', 'e0', 't0:4', 'z0:4', 'f0:2', 'f2:4')


def span(step):
    low, high = step[1:].split(":") if ":" in step else (step[1:], int(step[1:]) + 1)
    return int(low), int(high)


HALF_TOKENS = SEG // 2
HALF_MEM = MEM // 2
MESH = pl.DeviceIdType.MESH


def rope_tables(head):
    half = head // 2
    frequency = rope_base ** (-(np.arange(half, dtype=np.float64) * 2.0) / head)
    angles = np.arange(ROWS)[:, None] * frequency[None, :]
    cosine, sine = np.cos(angles), np.sin(angles)
    return (
        np.concatenate([cosine, cosine], axis=1).astype(np.float32),
        np.concatenate([-sine, sine], axis=1).astype(np.float32),
    )


def layer_kernel(
    len_ref, gain_ref, cos_ref, sin_ref, m0_ref, emb_ref, wq_ref, wk_ref, wv_ref, wo_ref,
    out_ref,
    wq_v, wk_v, wv_v, wo_v, xin, core_snd, core_rcv, tok_snd, tok_rcv, mem_snd, mem_rcv, newt,
    part, acc, mixed, gain_v, cos_v, sin_v,
    msem, esem, wsem, osem, ssem, send_sem, recv_sem,
):
    width = xin.shape[-1]
    half = width // 2
    q_cols, kv_cols = wq_v.shape[1], wk_v.shape[1]
    me = lax.axis_index("tp")
    group, rank = me // RANKS, me % RANKS
    xb, cb = rank // 2, rank % 2
    core_peer = group * RANKS + xb * 2 + (1 - cb)
    x_peer = group * RANKS + (1 - xb) * 2 + (1 - cb)
    has_next, has_prev = group < SECTIONS - 1, group > 0
    next_peer, prev_peer = me + RANKS, me - RANKS
    side = (rank // 2 + rank % 2) % 2
    own_rows = pl.ds(pl.multiple_of(MEM + xb * HALF_TOKENS, 16), HALF_TOKENS)
    far_rows = pl.ds(pl.multiple_of(MEM + (1 - xb) * HALF_TOKENS, 16), HALF_TOKENS)
    mem_rows = pl.ds(0, MEM)
    own_memory = pl.ds(pl.multiple_of(xb * HALF_MEM, 16), HALF_MEM)
    far_memory = pl.ds(pl.multiple_of((1 - xb) * HALF_MEM, 16), HALF_MEM)

    def reach(low, high=None):
        return STARTS[low], sum(WIDTHS[low : low + 1 if high is None else high])

    def own_cols(low, high=None):
        start, size = reach(low, high)
        return pl.ds(pl.multiple_of(side * half + start, 128), size)

    def peer_cols(low, high=None):
        start, size = reach(low, high)
        return pl.ds(pl.multiple_of((1 - side) * half + start, 128), size)

    def half_cols(low, high=None):
        return pl.ds(*reach(low, high))

    blocks_in = [(step[0] == "g", *span(step)) for step in GATHER if step[0] in "gh"]
    blocks_out = [(step[0] == "o", *span(step)) for step in FINISH if step[0] in "po"]
    memory_spans = dict(span(step) for step in FINISH if step[0] == "m")
    peer_out = {low: high for mine, low, high in blocks_out if not mine}

    def block_cols(mine, low, high):
        return own_cols(low, high) if mine else peer_cols(low, high)

    def weight_copies(o):
        cols = block_cols(*blocks_in[o])
        return [
            pltpu.make_async_copy(src.at[cols], dst.at[cols], wsem.at[i, o])
            for i, (src, dst) in enumerate(((wq_ref, wq_v), (wk_ref, wk_v), (wv_ref, wv_v)))
        ]

    def out_copy(o):
        cols = block_cols(*blocks_out[o])
        return pltpu.make_async_copy(wo_ref.at[:, cols], wo_v.at[:, cols], osem.at[o])

    def in_copy(k):
        return pltpu.make_async_copy(
            emb_ref.at[0, k], xin.at[k, pl.ds(MEM, SEG)], esem.at[k]
        )

    def remote(src, dst, kind, k, j, peer):
        return pltpu.make_async_remote_copy(
            src_ref=src, dst_ref=dst, send_sem=send_sem.at[kind, k, j],
            recv_sem=recv_sem.at[kind, k, j],
            device_id={"tp": peer}, device_id_type=MESH,
        )

    def in_place(ref, kind, k, j, peer):
        return remote(ref, ref, kind, k, j, peer)

    def z_copy(k, j):
        return remote(
            newt.at[k, :, own_cols(j)], xin.at[k, own_rows, own_cols(j)], 0, k, j, next_peer
        )

    def gather_x(k, j):
        return in_place(xin.at[k, own_rows, own_cols(j)], 1, k, j, x_peer)

    def gather_core(k, j):
        return in_place(xin.at[k, own_rows, own_cols(j)], 2, k, j, core_peer)

    def gather_far(k, j):
        return in_place(xin.at[k, far_rows, own_cols(j)], 3, k, j, core_peer)

    def sum_core(k, low):
        cols = half_cols(low, peer_out[low])
        return remote(core_snd.at[k, :, cols], core_rcv.at[k, :, cols], 4, k, low, core_peer)

    def sum_tokens(k, j):
        return remote(
            tok_snd.at[k, :, half_cols(j)], tok_rcv.at[k, :, half_cols(j)], 5, k, j, x_peer
        )

    def sum_memory(k, low):
        cols = half_cols(low, memory_spans[low])
        return remote(mem_snd.at[k, :, cols], mem_rcv.at[k, :, cols], 6, k, low, x_peer)

    def sum_last_memory(low):
        rows = (SEGS - 1, far_memory, half_cols(low, memory_spans[low]))
        return remote(mem_snd.at[*rows], mem_rcv.at[*rows], 6, SEGS - 1, low, x_peer)

    def last_memory(low):
        cols = own_cols(low, memory_spans[low])
        return in_place(xin.at[SEGS, own_memory, cols], 7, SEGS - 1, low, core_peer)

    def next_memory(k, low):
        cols = own_cols(low, memory_spans[low])
        return in_place(xin.at[k + 1, mem_rows, cols], 7, k, low, core_peer)

    def out_tokens(k):
        return in_place(newt.at[k, :, own_cols(0, CHUNKS)], 8, k, 0, core_peer)

    first_memory = pltpu.make_async_copy(m0_ref.at[group], xin.at[0, mem_rows], msem)
    gain_copy = pltpu.make_async_copy(gain_ref, gain_v, ssem.at[0])
    cos_copy = pltpu.make_async_copy(cos_ref, cos_v, ssem.at[1])
    sin_copy = pltpu.make_async_copy(sin_ref, sin_v, ssem.at[2])

    def start_weights(o):
        for copy in weight_copies(o):
            copy.start()

    @pl.when(group == 0)
    def _():
        in_copy(0).start()

    first_memory.start()
    gain_copy.start()
    start_weights(0)
    start_weights(1)

    barrier = pltpu.get_barrier_semaphore()
    for peer in (core_peer, x_peer):
        pl.semaphore_signal(barrier, inc=1, device_id={"tp": peer}, device_id_type=MESH)

    @pl.when(has_next)
    def _():
        pl.semaphore_signal(barrier, inc=1, device_id={"tp": next_peer}, device_id_type=MESH)

    @pl.when(has_prev)
    def _():
        pl.semaphore_signal(barrier, inc=1, device_id={"tp": prev_peer}, device_id_type=MESH)

    for o in range(2, len(blocks_in)):
        start_weights(o)
    cos_copy.start()
    sin_copy.start()
    for o in range(len(blocks_out)):
        out_copy(o).start()

    @pl.when(group == 0)
    def _():
        for k in range(1, SEGS):
            in_copy(k).start()

    inner = has_next & has_prev

    @pl.when(inner)
    def _():
        pl.semaphore_wait(barrier, 4)

    @pl.when(has_prev & jnp.logical_not(has_next))
    def _():
        pl.semaphore_wait(barrier, 3)

    first_memory.wait()
    gain_copy.wait()

    def pass_on(k, j):
        @pl.when(has_prev)
        def _():
            z_copy(k, j).wait_recv()
            gather_x(k, j).start()
            gather_core(k, j).start()

    def pass_far(k, j):
        @pl.when(has_prev)
        def _():
            gather_x(k, j).wait_recv()
            gather_far(k, j).start()

    def rope(block):
        return block * cos_v[...] + pltpu.roll(block, HD // 2, 1) * sin_v[...]

    def emit_out(k):
        length = len_ref[0, k]
        step = half // 4
        row = lax.broadcasted_iota(jnp.int32, (32, step), 0)
        kept = (row < 8) | (xb * HALF_TOKENS + cb * 24 + row - 8 < length)
        for j in range(8):
            cols = pl.ds(j * step, step)
            memory = xin[k + 1, mem_rows, cols].astype(jnp.float32)
            tokens = newt[k, :, cols].astype(jnp.float32)
            low = jnp.where(xb == 0, memory[:16], memory[16:])
            block = jnp.concatenate(
                [
                    jnp.where(cb == 0, low[:8], low[8:]),
                    jnp.where(cb == 0, tokens[:24], tokens[24:]),
                ],
                axis=0,
            )
            out_ref[0, k, :, cols] = jnp.where(kept, block, 0.0).astype(jnp.bfloat16)

    def segment(k, carry):
        length = len_ref[0, k]
        squares = jnp.zeros((ROWS, 1), jnp.float32)

        @pl.when(group == 0)
        def _():
            in_copy(k).wait()

        o = 0
        for step in GATHER:
            kind, (j, last) = step[0], span(step)
            if kind == "z":
                pass_on(k, j)
                continue
            if kind == "x":
                pass_far(k, j)
                continue
            if kind == "h":

                @pl.when(has_prev)
                def _():
                    for i in range(j, last):
                        gather_core(k, i).wait_recv()
                        gather_far(k, i).wait_recv()

                @pl.when(k > 0)
                def _():
                    for i in range(j, last):
                        if i in memory_spans:
                            next_memory(k - 1, i).wait_recv()

            @pl.when(k == 0)
            def _():
                for copy in weight_copies(o):
                    copy.wait()

            cols = block_cols(*blocks_in[o])
            raw = xin[k, :, cols].astype(jnp.float32)
            squares = squares + jnp.sum(raw * raw, axis=1, keepdims=True)
            gained = (raw * gain_v[pl.ds(group, 1), cols]).astype(jnp.bfloat16)
            low = 0
            for weight in (wq_v, wk_v, wv_v):
                high = low + weight.shape[1]
                term = jnp.dot(gained, weight[cols], preferred_element_type=jnp.float32)
                if o == 0:
                    acc[:, low:high] = term
                else:
                    acc[:, low:high] += term
                low = high
            o += 1

        @pl.when(k == 0)
        def _():
            cos_copy.wait()
            sin_copy.wait()

        @pl.when((k == 0) & (group == 0))
        def _():
            pl.semaphore_wait(barrier, 3)

        factor = lax.rsqrt(squares * (1.0 / width) + eps)
        query_pos = lax.broadcasted_iota(jnp.int32, (ROWS, ROWS), 0)
        key_pos = lax.broadcasted_iota(jnp.int32, (ROWS, ROWS), 1)
        real_key = (key_pos < MEM) | (key_pos - MEM < length)
        ordered = (key_pos <= query_pos) | (query_pos < MEM)
        bias = jnp.where(real_key & ordered, 0.0, -1e30).astype(jnp.float32)
        per_kv = q_cols // kv_cols
        for g in range(kv_cols // HD):
            key_raw = (acc[:, q_cols + g * HD : q_cols + (g + 1) * HD] * factor).astype(
                jnp.bfloat16
            )
            key = rope(key_raw.astype(jnp.float32)).astype(jnp.bfloat16)
            low = q_cols + kv_cols + g * HD
            value = (acc[:, low : low + HD] * factor).astype(jnp.bfloat16)
            heads = range(g * per_kv, (g + 1) * per_kv)
            queries = jnp.concatenate(
                [
                    rope(acc[:, h * HD : (h + 1) * HD] * factor).astype(jnp.bfloat16)
                    for h in heads
                ],
                axis=0,
            )
            scores = lax.dot_general(
                queries, key, (((1,), (1,)), ((), ())), preferred_element_type=jnp.float32
            ) * HD ** (-0.5)
            scores = scores.reshape(per_kv, ROWS, ROWS) + bias[None]
            weight = jnp.exp(scores - jnp.max(scores, axis=2, keepdims=True))
            share = 1.0 / jnp.sum(weight, axis=2, keepdims=True)
            blended = jnp.dot(
                weight.astype(jnp.bfloat16).reshape(per_kv * ROWS, ROWS),
                value,
                preferred_element_type=jnp.float32,
            ).reshape(per_kv, ROWS, HD) * share
            for i, h in enumerate(heads):
                mixed[:, h * HD : (h + 1) * HD] = blended[i].astype(jnp.bfloat16)

        def project_peer(low, high):
            @pl.when(k == 0)
            def _():
                out_copy(blocks_out.index((False, low, high))).wait()

            term = jnp.dot(
                mixed[...], wo_v[:, peer_cols(low, high)], preferred_element_type=jnp.float32
            )
            core_snd[k, :, half_cols(low, high)] = term.astype(jnp.bfloat16)
            sum_core(k, low).start()

        def project_own(low, high):
            @pl.when(k == 0)
            def _():
                out_copy(blocks_out.index((True, low, high))).wait()

            part[:, half_cols(low, high)] = jnp.dot(
                mixed[...], wo_v[:, own_cols(low, high)], preferred_element_type=jnp.float32
            )

        def cross(j):
            if j in peer_out:
                sum_core(k, j).wait_recv()
            cols = half_cols(j)
            far = part[far_rows, cols] + core_rcv[k, far_rows, cols].astype(jnp.float32)
            tok_snd[k, :, cols] = far.astype(jnp.bfloat16)
            sum_tokens(k, j).start()
            part[own_rows, cols] = (
                part[own_rows, cols]
                + core_rcv[k, own_rows, cols].astype(jnp.float32)
                + xin[k, own_rows, own_cols(j)].astype(jnp.float32)
            )

        def cross_memory(low, high):
            cols = half_cols(low, high)
            memory = part[mem_rows, cols] + core_rcv[k, mem_rows, cols].astype(jnp.float32)
            mem_snd[k, :, cols] = memory.astype(jnp.bfloat16)

            @pl.when(k + 1 < SEGS)
            def _():
                sum_memory(k, low).start()

            @pl.when(k + 1 == SEGS)
            def _():
                sum_last_memory(low).start()

            part[mem_rows, cols] = memory + xin[k, mem_rows, own_cols(low, high)].astype(jnp.float32)

        def finish_tokens(j):
            sum_tokens(k, j).wait_recv()
            cols = half_cols(j)
            state = part[own_rows, cols] + tok_rcv[k, :, cols].astype(jnp.float32)
            newt[k, :, own_cols(j)] = state.astype(jnp.bfloat16)

            @pl.when(has_next)
            def _():
                z_copy(k, j).start()

            if j == CHUNKS - 1:
                out_tokens(k).start()

        def finish_memory(low, high):
            cols = half_cols(low, high)

            @pl.when(k + 1 < SEGS)
            def _():
                sum_memory(k, low).wait_recv()
                state = part[mem_rows, cols] + mem_rcv[k, :, cols].astype(jnp.float32)
                xin[k + 1, mem_rows, own_cols(low, high)] = state.astype(jnp.bfloat16)
                next_memory(k, low).start()

            @pl.when(k + 1 == SEGS)
            def _():
                sum_last_memory(low).wait_recv()
                got = mem_rcv[SEGS - 1, own_memory, cols].astype(jnp.float32)
                state = part[own_memory, cols] + got
                xin[SEGS, own_memory, own_cols(low, high)] = state.astype(jnp.bfloat16)
                last_memory(low).start()

        def emit_last(j):
            @pl.when(k > 0)
            def _():
                out_tokens(k - 1).wait_recv()
                emit_out(k - 1)

        def pass_next(j):
            @pl.when(k + 1 < SEGS)
            def _():
                pass_on(k + 1, j)

        def pass_far_next(j):
            @pl.when(k + 1 < SEGS)
            def _():
                pass_far(k + 1, j)

        actions = {
            "p": project_peer, "o": project_own, "c": cross, "m": cross_memory,
            "t": finish_tokens, "f": finish_memory, "e": emit_last, "z": pass_next,
            "x": pass_far_next,
        }
        for step in FINISH:
            if step[0] in "pomf":
                actions[step[0]](*span(step))
            else:
                for j in range(*span(step)):
                    actions[step[0]](j)
        return carry

    for j in range(CHUNKS):
        pass_on(0, j)
    lax.fori_loop(0, SEGS, segment, 0)
    out_tokens(SEGS - 1).wait_recv()
    for low in memory_spans:
        last_memory(low).wait_recv()
    emit_out(SEGS - 1)

    def drain(k, carry):
        for low in peer_out:
            sum_core(k, low).wait_send()
        out_tokens(k).wait_send()
        for low in memory_spans:

            @pl.when(k + 1 < SEGS)
            def _():
                sum_memory(k, low).wait_send()
                next_memory(k, low).wait_send()

            @pl.when(k + 1 == SEGS)
            def _():
                sum_last_memory(low).wait_send()
                last_memory(low).wait_send()

        for j in range(CHUNKS):
            sum_tokens(k, j).wait_send()

            @pl.when(has_next)
            def _():
                z_copy(k, j).wait_send()

            @pl.when(has_prev)
            def _():
                gather_x(k, j).wait_send()
                gather_core(k, j).wait_send()
                gather_far(k, j).wait_send()


        return carry

    lax.fori_loop(0, SEGS, drain, 0)


def streamed(embeddings, lengths, mem_init, norm_gain, w_query, w_key, w_value, w_out):
    width = embeddings.shape[-1]
    q_cols, kv_cols = w_query.shape[1], w_key.shape[1]
    cosine, sine = rope_tables(HD)
    anywhere = pl.BlockSpec(memory_space=pl.ANY)
    dma = pltpu.SemaphoreType.DMA
    half = jnp.bfloat16
    return pl.pallas_call(
        layer_kernel,
        out_shape=pltpu.VMEM((1, SEGS, 32, width), half),
        in_specs=[pl.BlockSpec(memory_space=pltpu.SMEM)] + [anywhere] * 9,
        out_specs=pl.BlockSpec(memory_space=pltpu.VMEM),
        scratch_shapes=[
            pltpu.VMEM((width, q_cols), half),
            pltpu.VMEM((width, kv_cols), half),
            pltpu.VMEM((width, kv_cols), half),
            pltpu.VMEM((q_cols, width), half),
            pltpu.VMEM((SEGS + 1, ROWS, width), half),
            pltpu.VMEM((SEGS, ROWS, width // 2), half),
            pltpu.VMEM((SEGS, ROWS, width // 2), half),
            pltpu.VMEM((SEGS, HALF_TOKENS, width // 2), half),
            pltpu.VMEM((SEGS, HALF_TOKENS, width // 2), half),
            pltpu.VMEM((SEGS, MEM, width // 2), half),
            pltpu.VMEM((SEGS, MEM, width // 2), half),
            pltpu.VMEM((SEGS, HALF_TOKENS, width), half),
            pltpu.VMEM((ROWS, width // 2), jnp.float32),
            pltpu.VMEM((ROWS, q_cols + 2 * kv_cols), jnp.float32),
            pltpu.VMEM((ROWS, q_cols), half),
            pltpu.VMEM(norm_gain.shape, jnp.float32),
            pltpu.VMEM((ROWS, HD), jnp.float32),
            pltpu.VMEM((ROWS, HD), jnp.float32),
            dma,
            dma((SEGS,)),
            dma((3, 2 * CHUNKS)),
            dma((2 * CHUNKS,)),
            dma((3,)),
            dma((9, SEGS, CHUNKS)),
            dma((9, SEGS, CHUNKS)),
        ],
        compiler_params=pltpu.CompilerParams(
            collective_id=0, has_side_effects=True, vmem_limit_bytes=56 * 2**20
        ),
    )(
        lengths, norm_gain, jnp.asarray(cosine), jnp.asarray(sine), mem_init, embeddings,
        w_query, w_key, w_value, w_out,
    )


def solution(mesh):
    in_specs = (
        P("parts", None, None, None),
        P("parts", None),
        P(),
        P(),
        P(None, "tp"),
        P(None, "tp"),
        P(None, "tp"),
        P("tp", None),
    )
    out_specs = P("tp", "parts", None, None)
    body = streamed if mesh.shape["tp"] == SECTIONS * RANKS else local
    return jax.shard_map(body, mesh=mesh, in_specs=in_specs, out_specs=out_specs, check_vma=False)
```

```python
import jax
import jax.numpy as jnp
import numpy as np
from jax import lax
from jax.experimental import pallas as pl
from jax.experimental.pallas import tpu as pltpu
from jax.sharding import PartitionSpec as P

HD = 128
MEM = 32
SECTIONS = 4
SEGS = 3
SEG = 96


eps = 1e-05
rope_base = 500000.0


def from_partner(block, axis, bit):
    count = lax.axis_size(axis)
    route = []
    for low in range(count):
        high = low | 1 << bit
        if high != low and high < count:
            route += [(low, high), (high, low)]
    return lax.ppermute(block, axis, route)


def shortened(value):
    return jax.tree.map(lambda a: a.astype(jnp.bfloat16) if a.dtype == jnp.float32 else a, value)


def shifted(value, axis, by):
    peers = lax.axis_size(axis)
    pairs = [(i, i + by) for i in range(peers) if 0 <= i + by < peers]
    return lax.ppermute(value, axis, pairs)


def rotate(heads_in, positions):
    half_size = heads_in.shape[-1] // 2
    frequency = rope_base ** (
        -(jnp.arange(half_size, dtype=jnp.float32) * 2.0) / heads_in.shape[-1]
    )
    angles = positions.astype(jnp.float32)[:, None] * frequency[None, :]
    cosine = jnp.cos(angles)[:, None, :]
    sine_part = jnp.sin(angles)[:, None, :]
    first_half = heads_in[..., :half_size]
    second_half = heads_in[..., half_size:]
    return jnp.concatenate(
        [
            first_half * cosine - second_half * sine_part,
            second_half * cosine + first_half * sine_part,
        ],
        axis=-1,
    )


def visible(positions, length):
    query_ids = positions[:, None]
    key_ids = positions[None, :]
    real_key = (key_ids < MEM) | (key_ids - MEM < length)
    ordered = (key_ids <= query_ids) | (query_ids < MEM)
    return real_key & ordered


def normalize(widened, gain_row):
    scaled = widened * lax.rsqrt(jnp.mean(widened * widened, axis=-1, keepdims=True) + eps)
    return (scaled * gain_row).astype(jnp.bfloat16)


def attend(queries, key_heads, value_heads, positions, length):
    row_total = queries.shape[0]
    kv_local = key_heads.shape[1]
    grouped = queries.reshape(row_total, kv_local, -1, queries.shape[-1])
    scores = jnp.einsum(
        "qgrd,kgd->grqk", grouped, key_heads, preferred_element_type=jnp.float32
    ) * HD ** (-0.5)
    scores = jnp.where(visible(positions, length)[None, None], scores, -1e30)
    softmaxed = jax.nn.softmax(scores, axis=-1).astype(jnp.bfloat16)
    mixed = jnp.einsum(
        "grqk,kgd->qgrd", softmaxed, value_heads, preferred_element_type=jnp.float32
    ).astype(jnp.bfloat16)
    return mixed.reshape(row_total, -1)


def finish(widened, summed_out, length, row_ids):
    new_state = (widened + summed_out).astype(jnp.bfloat16)
    kept_rows = (row_ids < MEM) | (row_ids - MEM < length)
    return jnp.where(kept_rows[:, None], new_state, jnp.zeros_like(new_state))


def order_pair(mine, partner, lower_half):
    first_part = jnp.where(lower_half, mine, partner)
    second_part = jnp.where(lower_half, partner, mine)
    return jnp.concatenate([first_part, second_part], axis=0)


def gather_rows(piece, my_rank, seq_bits, rank_bits, level_list):
    stacked = piece
    for rank_bit in level_list:
        partner = from_partner(stacked, "tp", seq_bits + rank_bit)
        upper_half = my_rank // 2**rank_bit % 2 == 1
        stacked = jnp.where(
            upper_half, jnp.stack([partner, stacked], axis=0), jnp.stack([stacked, partner], axis=0)
        )
    axis_bits = list(reversed(level_list))
    order_axes = [axis_bits.index(rank_bit) for rank_bit in reversed(range(rank_bits))]
    stacked = jnp.transpose(stacked, order_axes + [rank_bits, rank_bits + 1])
    return stacked.reshape(2**rank_bits * piece.shape[0], piece.shape[-1])


def scatter_rows(partial_term, my_rank, seq_bits, rank_bits, level_list, shard_rows):
    model_width = partial_term.shape[-1]
    running = partial_term.reshape((2,) * rank_bits + (shard_rows, model_width))
    axis_bits = list(reversed(range(rank_bits)))
    for rank_bit in level_list:
        position = axis_bits.index(rank_bit)
        upper_half = my_rank // 2**rank_bit % 2 == 1
        low_part = lax.index_in_dim(running, 0, position, keepdims=False)
        high_part = lax.index_in_dim(running, 1, position, keepdims=False)
        kept_rows = jnp.where(upper_half, high_part, low_part)
        sent_rows = jnp.where(upper_half, low_part, high_part)
        running = kept_rows + from_partner(
            sent_rows.astype(jnp.bfloat16), "tp", seq_bits + rank_bit
        ).astype(sent_rows.dtype)
        axis_bits = [other_bit for other_bit in axis_bits if other_bit != rank_bit]
    return running


def local(embeddings, lengths, mem_init, norm_gain, w_query, w_key, w_value, w_out):
    axis_width = lax.axis_size("tp")
    group_size = axis_width // SECTIONS
    rank_count = min(8, group_size)
    seq_count = group_size // rank_count
    seq_bits = seq_count.bit_length() - 1
    rank_bits = rank_count.bit_length() - 1
    device_index = lax.axis_index("tp")
    group_index = device_index // group_size
    my_rank = device_index % group_size // seq_count
    my_seq = device_index % seq_count
    model_width = embeddings.shape[-1]
    row_total = SEG + MEM
    shard_rows = row_total // rank_count
    mem_block = MEM // rank_count
    token_block = SEG // rank_count
    within = jnp.arange(shard_rows, dtype=jnp.int32)
    block_ids = jnp.arange(rank_count, dtype=jnp.int32)[:, None]
    positions = jnp.where(
        within[None, :] < mem_block,
        block_ids * mem_block + within[None, :],
        MEM + block_ids * token_block + within[None, :] - mem_block,
    ).reshape(-1)
    row_ids = lax.dynamic_index_in_dim(
        positions.reshape(rank_count, shard_rows), my_rank, 0, keepdims=False
    )
    gain_row = lax.dynamic_index_in_dim(norm_gain, group_index, 0, keepdims=False)
    my_lengths = lax.dynamic_index_in_dim(lengths, my_seq, 0, keepdims=False)
    first_memory = lax.dynamic_slice(
        mem_init, (group_index, my_rank * mem_block, 0), (1, mem_block, model_width)
    ).reshape(mem_block, model_width)
    query_stack, key_stack, value_stack, out_stack = (
        w_query[None],
        w_key[None],
        w_value[None],
        w_out[None],
    )
    for seq_bit in range(seq_bits):
        partner_query, partner_key, partner_value, partner_out = (
            from_partner(shortened(query_stack), "tp", seq_bit).astype(query_stack.dtype),
            from_partner(shortened(key_stack), "tp", seq_bit).astype(key_stack.dtype),
            from_partner(shortened(value_stack), "tp", seq_bit).astype(value_stack.dtype),
            from_partner(shortened(out_stack), "tp", seq_bit).astype(out_stack.dtype),
        )
        lower_half = device_index // 2**seq_bit % 2 == 0
        query_stack = order_pair(query_stack, partner_query, lower_half)
        key_stack = order_pair(key_stack, partner_key, lower_half)
        value_stack = order_pair(value_stack, partner_value, lower_half)
        out_stack = order_pair(out_stack, partner_out, lower_half)
    level_list = list(range(rank_bits))
    states = jnp.zeros((SEGS, shard_rows, model_width), jnp.bfloat16)
    memory = jnp.zeros((mem_block, model_width), jnp.bfloat16)
    arrived = jnp.zeros((token_block, model_width), jnp.bfloat16)
    step_total = SEGS + SECTIONS - 1
    for step_index in range(step_total):
        segment = step_index - group_index
        active = (segment >= 0) & (segment < SEGS)
        clipped = jnp.clip(segment, 0, SEGS - 1)
        length = lax.dynamic_index_in_dim(my_lengths, clipped, 0, keepdims=False)
        embedded = lax.dynamic_slice(
            embeddings,
            (my_seq, clipped, my_rank * token_block, 0),
            (1, 1, token_block, model_width),
        ).reshape(token_block, model_width)
        token_source = jnp.where(group_index == 0, embedded, arrived)
        memory_source = jnp.where(segment == 0, first_memory, memory)
        inputs = jnp.concatenate([memory_source, token_source], axis=0)
        widened = inputs.astype(jnp.float32)
        normed = normalize(widened, gain_row)
        gathered = gather_rows(normed, my_rank, seq_bits, rank_bits, level_list)
        query_all = jnp.einsum(
            "rd,sdc->rsc", gathered, query_stack, preferred_element_type=jnp.float32
        )
        queries = rotate(query_all.reshape(row_total, -1, HD), positions).astype(jnp.bfloat16)
        key_all = jnp.einsum("rd,sdc->rsc", gathered, key_stack, preferred_element_type=jnp.float32)
        key_raw = lax.optimization_barrier(key_all.reshape(row_total, -1).astype(jnp.bfloat16))
        value_all = jnp.einsum(
            "rd,sdc->rsc", gathered, value_stack, preferred_element_type=jnp.float32
        ).astype(jnp.bfloat16)
        key_heads = rotate(
            key_raw.astype(jnp.float32).reshape(row_total, -1, HD), positions
        ).astype(jnp.bfloat16)
        value_heads = value_all.reshape(row_total, -1, HD)
        mixed_heads = attend(queries, key_heads, value_heads, positions, length)
        mixed_split = mixed_heads.reshape(row_total, out_stack.shape[0], out_stack.shape[1])
        partial_term = jnp.einsum(
            "rsc,scd->rd", mixed_split, out_stack, preferred_element_type=jnp.float32
        )
        summed_out = scatter_rows(
            partial_term, my_rank, seq_bits, rank_bits, level_list, shard_rows
        )
        new_state = finish(widened, summed_out, length, row_ids)
        memory = jnp.where(active, new_state[:mem_block], memory)
        states = jnp.where(
            active, lax.dynamic_update_index_in_dim(states, new_state, clipped, 0), states
        )
        if step_index + 1 < step_total:
            arrived = shifted(new_state[mem_block:], "tp", group_size)
    return states[None]


RANKS = 4
WIDTHS = (512, 512, 512, 512)
STARTS = tuple(sum(WIDTHS[:j]) for j in range(len(WIDTHS)))
CHUNKS = len(WIDTHS)
ROWS = SEG + MEM
GATHER = ('x0', 'g0', 'x1', 'g1', 'x2', 'h0', 'g2', 'x3', 'h1', 'g3', 'h2', 'h3')
FINISH = ('p0', 'o0', 'p1', 'o1', 'c0', 'p2', 'o2', 'c1', 'p3', 'o3', 'c2:4', 'm0:2', 'm2:4', 'e0', 't0:4', 'z0:4', 'f0:2', 'f2:4')


LATE = {2: range(2), 3: range(2, 4), 4: range(4, 6), 5: range(6, 8)}


def span(step):
    low, high = step[1:].split(":") if ":" in step else (step[1:], int(step[1:]) + 1)
    return int(low), int(high)


HALF_TOKENS = SEG // 2
HALF_MEM = MEM // 2
MESH = pl.DeviceIdType.MESH


def rope_tables(head):
    half = head // 2
    frequency = rope_base ** (-(np.arange(half, dtype=np.float64) * 2.0) / head)
    angles = np.arange(ROWS)[:, None] * frequency[None, :]
    cosine, sine = np.cos(angles), np.sin(angles)
    return (
        np.concatenate([cosine, cosine], axis=1).astype(np.float32),
        np.concatenate([-sine, sine], axis=1).astype(np.float32),
    )


def layer_kernel(
    len_ref, gain_ref, cos_ref, sin_ref, m0_ref, emb_ref, wq_ref, wk_ref, wv_ref, wo_ref,
    out_ref,
    wq_v, wk_v, wv_v, wo_v, xin, core_snd, core_rcv, tok_snd, tok_rcv, mem_snd, mem_rcv, newt,
    part, acc, mixed, gain_v, cos_v, sin_v,
    msem, esem, wsem, osem, ssem, send_sem, recv_sem,
):
    width = xin.shape[-1]
    half = width // 2
    q_cols, kv_cols = wq_v.shape[1], wk_v.shape[1]
    me = lax.axis_index("tp")
    group, rank = me // RANKS, me % RANKS
    xb, cb = rank // 2, rank % 2
    core_peer = group * RANKS + xb * 2 + (1 - cb)
    x_peer = group * RANKS + (1 - xb) * 2 + (1 - cb)
    has_next, has_prev = group < SECTIONS - 1, group > 0
    next_peer, prev_peer = me + RANKS, me - RANKS
    side = (rank // 2 + rank % 2) % 2
    own_rows = pl.ds(pl.multiple_of(MEM + xb * HALF_TOKENS, 16), HALF_TOKENS)
    far_rows = pl.ds(pl.multiple_of(MEM + (1 - xb) * HALF_TOKENS, 16), HALF_TOKENS)
    mem_rows = pl.ds(0, MEM)
    own_memory = pl.ds(pl.multiple_of(xb * HALF_MEM, 16), HALF_MEM)
    far_memory = pl.ds(pl.multiple_of((1 - xb) * HALF_MEM, 16), HALF_MEM)

    def reach(low, high=None):
        return STARTS[low], sum(WIDTHS[low : low + 1 if high is None else high])

    def own_cols(low, high=None):
        start, size = reach(low, high)
        return pl.ds(pl.multiple_of(side * half + start, 128), size)

    def peer_cols(low, high=None):
        start, size = reach(low, high)
        return pl.ds(pl.multiple_of((1 - side) * half + start, 128), size)

    def half_cols(low, high=None):
        return pl.ds(*reach(low, high))

    blocks_in = [(step[0] == "g", *span(step)) for step in GATHER if step[0] in "gh"]
    blocks_out = [(step[0] == "o", *span(step)) for step in FINISH if step[0] in "po"]
    memory_spans = dict(span(step) for step in FINISH if step[0] == "m")
    peer_out = {low: high for mine, low, high in blocks_out if not mine}

    def block_cols(mine, low, high):
        return own_cols(low, high) if mine else peer_cols(low, high)

    def weight_copies(o):
        cols = block_cols(*blocks_in[o])
        return [
            pltpu.make_async_copy(src.at[cols], dst.at[cols], wsem.at[i, o])
            for i, (src, dst) in enumerate(((wq_ref, wq_v), (wk_ref, wk_v), (wv_ref, wv_v)))
        ]

    def out_copy(o):
        cols = block_cols(*blocks_out[o])
        return pltpu.make_async_copy(wo_ref.at[:, cols], wo_v.at[:, cols], osem.at[o])

    def in_copy(k):
        return pltpu.make_async_copy(
            emb_ref.at[0, k], xin.at[k, pl.ds(MEM, SEG)], esem.at[k]
        )

    def remote(src, dst, kind, k, j, peer):
        return pltpu.make_async_remote_copy(
            src_ref=src, dst_ref=dst, send_sem=send_sem.at[kind, k, j],
            recv_sem=recv_sem.at[kind, k, j],
            device_id={"tp": peer}, device_id_type=MESH,
        )

    def in_place(ref, kind, k, j, peer):
        return remote(ref, ref, kind, k, j, peer)

    def z_copy(k, j):
        return remote(
            newt.at[k, :, own_cols(j)], xin.at[k, own_rows, own_cols(j)], 0, k, j, next_peer
        )

    def gather_x(k, j):
        return in_place(xin.at[k, own_rows, own_cols(j)], 1, k, j, x_peer)

    def gather_core(k, j):
        return in_place(xin.at[k, own_rows, own_cols(j)], 2, k, j, core_peer)

    def gather_far(k, j):
        return in_place(xin.at[k, far_rows, own_cols(j)], 3, k, j, core_peer)

    def sum_core(k, low):
        cols = half_cols(low, peer_out[low])
        return remote(core_snd.at[k, :, cols], core_rcv.at[k, :, cols], 4, k, low, core_peer)

    def sum_tokens(k, j):
        return remote(
            tok_snd.at[k, :, half_cols(j)], tok_rcv.at[k, :, half_cols(j)], 5, k, j, x_peer
        )

    def sum_memory(k, low):
        cols = half_cols(low, memory_spans[low])
        return remote(mem_snd.at[k, :, cols], mem_rcv.at[k, :, cols], 6, k, low, x_peer)

    def sum_last_memory(low):
        rows = (SEGS - 1, far_memory, half_cols(low, memory_spans[low]))
        return remote(mem_snd.at[*rows], mem_rcv.at[*rows], 6, SEGS - 1, low, x_peer)

    def last_memory(low):
        cols = own_cols(low, memory_spans[low])
        return in_place(xin.at[SEGS, own_memory, cols], 7, SEGS - 1, low, core_peer)

    def next_memory(k, low):
        cols = own_cols(low, memory_spans[low])
        return in_place(xin.at[k + 1, mem_rows, cols], 7, k, low, core_peer)

    def out_tokens(k):
        return in_place(newt.at[k, :, own_cols(0, CHUNKS)], 8, k, 0, core_peer)

    first_memory = pltpu.make_async_copy(m0_ref.at[group], xin.at[0, mem_rows], msem)
    gain_copy = pltpu.make_async_copy(gain_ref, gain_v, ssem.at[0])
    cos_copy = pltpu.make_async_copy(cos_ref, cos_v, ssem.at[1])
    sin_copy = pltpu.make_async_copy(sin_ref, sin_v, ssem.at[2])

    def start_weights(o):
        for copy in weight_copies(o):
            copy.start()

    @pl.when(group == 0)
    def _():
        in_copy(0).start()

    first_memory.start()
    gain_copy.start()
    start_weights(0)
    start_weights(1)

    barrier = pltpu.get_barrier_semaphore()
    for peer in (core_peer, x_peer):
        pl.semaphore_signal(barrier, inc=1, device_id={"tp": peer}, device_id_type=MESH)

    @pl.when(has_next)
    def _():
        pl.semaphore_signal(barrier, inc=1, device_id={"tp": next_peer}, device_id_type=MESH)

    @pl.when(has_prev)
    def _():
        pl.semaphore_signal(barrier, inc=1, device_id={"tp": prev_peer}, device_id_type=MESH)

    for o in range(2, len(blocks_in)):
        start_weights(o)
    cos_copy.start()
    sin_copy.start()

    @pl.when(has_prev)
    def _():
        for o in range(len(blocks_out)):
            out_copy(o).start()

    @pl.when(group == 0)
    def _():
        for k in range(1, SEGS):
            in_copy(k).start()

    inner = has_next & has_prev

    @pl.when(inner)
    def _():
        pl.semaphore_wait(barrier, 4)

    @pl.when(has_prev & jnp.logical_not(has_next))
    def _():
        pl.semaphore_wait(barrier, 3)

    first_memory.wait()
    gain_copy.wait()

    def pass_on(k, j):
        @pl.when(has_prev)
        def _():
            z_copy(k, j).wait_recv()
            gather_x(k, j).start()
            gather_core(k, j).start()

    def pass_far(k, j):
        @pl.when(has_prev)
        def _():
            gather_x(k, j).wait_recv()
            gather_far(k, j).start()

    def rope(block):
        return block * cos_v[...] + pltpu.roll(block, HD // 2, 1) * sin_v[...]

    def emit_out(k):
        length = len_ref[0, k]
        step = half // 4
        row = lax.broadcasted_iota(jnp.int32, (32, step), 0)
        kept = (row < 8) | (xb * HALF_TOKENS + cb * 24 + row - 8 < length)
        for j in range(8):
            cols = pl.ds(j * step, step)
            memory = xin[k + 1, mem_rows, cols].astype(jnp.float32)
            tokens = newt[k, :, cols].astype(jnp.float32)
            low = jnp.where(xb == 0, memory[:16], memory[16:])
            block = jnp.concatenate(
                [
                    jnp.where(cb == 0, low[:8], low[8:]),
                    jnp.where(cb == 0, tokens[:24], tokens[24:]),
                ],
                axis=0,
            )
            out_ref[0, k, :, cols] = jnp.where(kept, block, 0.0).astype(jnp.bfloat16)

    def segment(k, carry):
        length = len_ref[0, k]
        squares = jnp.zeros((ROWS, 1), jnp.float32)

        @pl.when(group == 0)
        def _():
            in_copy(k).wait()

        o = 0
        for step in GATHER:
            kind, (j, last) = step[0], span(step)
            if kind == "z":
                pass_on(k, j)
                continue
            if kind == "x":
                pass_far(k, j)
                continue
            if kind == "h":

                @pl.when(has_prev)
                def _():
                    for i in range(j, last):
                        gather_core(k, i).wait_recv()
                        gather_far(k, i).wait_recv()

                @pl.when(k > 0)
                def _():
                    for i in range(j, last):
                        if i in memory_spans:
                            next_memory(k - 1, i).wait_recv()

            @pl.when(k == 0)
            def _():
                for copy in weight_copies(o):
                    copy.wait()

            if o in LATE:

                @pl.when((k == 0) & (group == 0))
                def _():
                    for i in LATE[o]:
                        out_copy(i).start()

            cols = block_cols(*blocks_in[o])
            raw = xin[k, :, cols].astype(jnp.float32)
            squares = squares + jnp.sum(raw * raw, axis=1, keepdims=True)
            gained = (raw * gain_v[pl.ds(group, 1), cols]).astype(jnp.bfloat16)
            low = 0
            for weight in (wq_v, wk_v, wv_v):
                high = low + weight.shape[1]
                term = jnp.dot(gained, weight[cols], preferred_element_type=jnp.float32)
                if o == 0:
                    acc[:, low:high] = term
                else:
                    acc[:, low:high] += term
                low = high
            o += 1

        @pl.when(k == 0)
        def _():
            cos_copy.wait()
            sin_copy.wait()

        @pl.when((k == 0) & (group == 0))
        def _():
            pl.semaphore_wait(barrier, 3)

        factor = lax.rsqrt(squares * (1.0 / width) + eps)
        query_pos = lax.broadcasted_iota(jnp.int32, (ROWS, ROWS), 0)
        key_pos = lax.broadcasted_iota(jnp.int32, (ROWS, ROWS), 1)
        real_key = (key_pos < MEM) | (key_pos - MEM < length)
        ordered = (key_pos <= query_pos) | (query_pos < MEM)
        bias = jnp.where(real_key & ordered, 0.0, -1e30).astype(jnp.float32)
        per_kv = q_cols // kv_cols
        for g in range(kv_cols // HD):
            key_raw = (acc[:, q_cols + g * HD : q_cols + (g + 1) * HD] * factor).astype(
                jnp.bfloat16
            )
            key = rope(key_raw.astype(jnp.float32)).astype(jnp.bfloat16)
            low = q_cols + kv_cols + g * HD
            value = (acc[:, low : low + HD] * factor).astype(jnp.bfloat16)
            heads = range(g * per_kv, (g + 1) * per_kv)
            queries = jnp.concatenate(
                [
                    rope(acc[:, h * HD : (h + 1) * HD] * factor).astype(jnp.bfloat16)
                    for h in heads
                ],
                axis=0,
            )
            scores = lax.dot_general(
                queries, key, (((1,), (1,)), ((), ())), preferred_element_type=jnp.float32
            ) * HD ** (-0.5)
            scores = scores.reshape(per_kv, ROWS, ROWS) + bias[None]
            weight = jnp.exp(scores - jnp.max(scores, axis=2, keepdims=True))
            share = 1.0 / jnp.sum(weight, axis=2, keepdims=True)
            blended = jnp.dot(
                weight.astype(jnp.bfloat16).reshape(per_kv * ROWS, ROWS),
                value,
                preferred_element_type=jnp.float32,
            ).reshape(per_kv, ROWS, HD) * share
            for i, h in enumerate(heads):
                mixed[:, h * HD : (h + 1) * HD] = blended[i].astype(jnp.bfloat16)

        def project_peer(low, high):
            @pl.when(k == 0)
            def _():
                out_copy(blocks_out.index((False, low, high))).wait()

            term = jnp.dot(
                mixed[...], wo_v[:, peer_cols(low, high)], preferred_element_type=jnp.float32
            )
            core_snd[k, :, half_cols(low, high)] = term.astype(jnp.bfloat16)
            sum_core(k, low).start()

        def project_own(low, high):
            @pl.when(k == 0)
            def _():
                out_copy(blocks_out.index((True, low, high))).wait()

            part[:, half_cols(low, high)] = jnp.dot(
                mixed[...], wo_v[:, own_cols(low, high)], preferred_element_type=jnp.float32
            )

        def cross(j):
            if j in peer_out:
                sum_core(k, j).wait_recv()
            cols = half_cols(j)
            far = part[far_rows, cols] + core_rcv[k, far_rows, cols].astype(jnp.float32)
            tok_snd[k, :, cols] = far.astype(jnp.bfloat16)
            sum_tokens(k, j).start()
            part[own_rows, cols] = (
                part[own_rows, cols]
                + core_rcv[k, own_rows, cols].astype(jnp.float32)
                + xin[k, own_rows, own_cols(j)].astype(jnp.float32)
            )

        def cross_memory(low, high):
            cols = half_cols(low, high)
            memory = part[mem_rows, cols] + core_rcv[k, mem_rows, cols].astype(jnp.float32)
            mem_snd[k, :, cols] = memory.astype(jnp.bfloat16)

            @pl.when(k + 1 < SEGS)
            def _():
                sum_memory(k, low).start()

            @pl.when(k + 1 == SEGS)
            def _():
                sum_last_memory(low).start()

            part[mem_rows, cols] = memory + xin[k, mem_rows, own_cols(low, high)].astype(jnp.float32)

        def finish_tokens(j):
            sum_tokens(k, j).wait_recv()
            cols = half_cols(j)
            state = part[own_rows, cols] + tok_rcv[k, :, cols].astype(jnp.float32)
            newt[k, :, own_cols(j)] = state.astype(jnp.bfloat16)

            @pl.when(has_next)
            def _():
                z_copy(k, j).start()

            if j == CHUNKS - 1:
                out_tokens(k).start()

        def finish_memory(low, high):
            cols = half_cols(low, high)

            @pl.when(k + 1 < SEGS)
            def _():
                sum_memory(k, low).wait_recv()
                state = part[mem_rows, cols] + mem_rcv[k, :, cols].astype(jnp.float32)
                xin[k + 1, mem_rows, own_cols(low, high)] = state.astype(jnp.bfloat16)
                next_memory(k, low).start()

            @pl.when(k + 1 == SEGS)
            def _():
                sum_last_memory(low).wait_recv()
                got = mem_rcv[SEGS - 1, own_memory, cols].astype(jnp.float32)
                state = part[own_memory, cols] + got
                xin[SEGS, own_memory, own_cols(low, high)] = state.astype(jnp.bfloat16)
                last_memory(low).start()

        def emit_last(j):
            @pl.when(k > 0)
            def _():
                out_tokens(k - 1).wait_recv()
                emit_out(k - 1)

        def pass_next(j):
            @pl.when(k + 1 < SEGS)
            def _():
                pass_on(k + 1, j)

        def pass_far_next(j):
            @pl.when(k + 1 < SEGS)
            def _():
                pass_far(k + 1, j)

        actions = {
            "p": project_peer, "o": project_own, "c": cross, "m": cross_memory,
            "t": finish_tokens, "f": finish_memory, "e": emit_last, "z": pass_next,
            "x": pass_far_next,
        }
        for step in FINISH:
            if step[0] in "pomf":
                actions[step[0]](*span(step))
            else:
                for j in range(*span(step)):
                    actions[step[0]](j)
        return carry

    for j in range(CHUNKS):
        pass_on(0, j)
    lax.fori_loop(0, SEGS, segment, 0)
    out_tokens(SEGS - 1).wait_recv()
    for low in memory_spans:
        last_memory(low).wait_recv()
    emit_out(SEGS - 1)

    def drain(k, carry):
        for low in peer_out:
            sum_core(k, low).wait_send()
        out_tokens(k).wait_send()
        for low in memory_spans:

            @pl.when(k + 1 < SEGS)
            def _():
                sum_memory(k, low).wait_send()
                next_memory(k, low).wait_send()

            @pl.when(k + 1 == SEGS)
            def _():
                sum_last_memory(low).wait_send()
                last_memory(low).wait_send()

        for j in range(CHUNKS):
            sum_tokens(k, j).wait_send()

            @pl.when(has_next)
            def _():
                z_copy(k, j).wait_send()

            @pl.when(has_prev)
            def _():
                gather_x(k, j).wait_send()
                gather_core(k, j).wait_send()
                gather_far(k, j).wait_send()


        return carry

    lax.fori_loop(0, SEGS, drain, 0)


def streamed(embeddings, lengths, mem_init, norm_gain, w_query, w_key, w_value, w_out):
    width = embeddings.shape[-1]
    q_cols, kv_cols = w_query.shape[1], w_key.shape[1]
    cosine, sine = rope_tables(HD)
    anywhere = pl.BlockSpec(memory_space=pl.ANY)
    dma = pltpu.SemaphoreType.DMA
    half = jnp.bfloat16
    return pl.pallas_call(
        layer_kernel,
        out_shape=pltpu.VMEM((1, SEGS, 32, width), half),
        in_specs=[pl.BlockSpec(memory_space=pltpu.SMEM)] + [anywhere] * 9,
        out_specs=pl.BlockSpec(memory_space=pltpu.VMEM),
        scratch_shapes=[
            pltpu.VMEM((width, q_cols), half),
            pltpu.VMEM((width, kv_cols), half),
            pltpu.VMEM((width, kv_cols), half),
            pltpu.VMEM((q_cols, width), half),
            pltpu.VMEM((SEGS + 1, ROWS, width), half),
            pltpu.VMEM((SEGS, ROWS, width // 2), half),
            pltpu.VMEM((SEGS, ROWS, width // 2), half),
            pltpu.VMEM((SEGS, HALF_TOKENS, width // 2), half),
            pltpu.VMEM((SEGS, HALF_TOKENS, width // 2), half),
            pltpu.VMEM((SEGS, MEM, width // 2), half),
            pltpu.VMEM((SEGS, MEM, width // 2), half),
            pltpu.VMEM((SEGS, HALF_TOKENS, width), half),
            pltpu.VMEM((ROWS, width // 2), jnp.float32),
            pltpu.VMEM((ROWS, q_cols + 2 * kv_cols), jnp.float32),
            pltpu.VMEM((ROWS, q_cols), half),
            pltpu.VMEM(norm_gain.shape, jnp.float32),
            pltpu.VMEM((ROWS, HD), jnp.float32),
            pltpu.VMEM((ROWS, HD), jnp.float32),
            dma,
            dma((SEGS,)),
            dma((3, 2 * CHUNKS)),
            dma((2 * CHUNKS,)),
            dma((3,)),
            dma((9, SEGS, CHUNKS)),
            dma((9, SEGS, CHUNKS)),
        ],
        compiler_params=pltpu.CompilerParams(
            collective_id=0, has_side_effects=True, vmem_limit_bytes=56 * 2**20
        ),
    )(
        lengths, norm_gain, jnp.asarray(cosine), jnp.asarray(sine), mem_init, embeddings,
        w_query, w_key, w_value, w_out,
    )


def solution(mesh):
    in_specs = (
        P("parts", None, None, None),
        P("parts", None),
        P(),
        P(),
        P(None, "tp"),
        P(None, "tp"),
        P(None, "tp"),
        P("tp", None),
    )
    out_specs = P("tp", "parts", None, None)
    body = streamed if mesh.shape["tp"] == SECTIONS * RANKS else local
    return jax.shard_map(body, mesh=mesh, in_specs=in_specs, out_specs=out_specs, check_vma=False)
```

```python
import jax
import jax.numpy as jnp
import numpy as np
from jax import lax
from jax.experimental import pallas as pl
from jax.experimental.pallas import tpu as pltpu
from jax.sharding import PartitionSpec as P

HD = 128
MEM = 32
SECTIONS = 4
SEGS = 3
SEG = 96


eps = 1e-05
rope_base = 500000.0


def from_partner(block, axis, bit):
    count = lax.axis_size(axis)
    route = []
    for low in range(count):
        high = low | 1 << bit
        if high != low and high < count:
            route += [(low, high), (high, low)]
    return lax.ppermute(block, axis, route)


def shortened(value):
    return jax.tree.map(lambda a: a.astype(jnp.bfloat16) if a.dtype == jnp.float32 else a, value)


def shifted(value, axis, by):
    peers = lax.axis_size(axis)
    pairs = [(i, i + by) for i in range(peers) if 0 <= i + by < peers]
    return lax.ppermute(value, axis, pairs)


def rotate(heads_in, positions):
    half_size = heads_in.shape[-1] // 2
    frequency = rope_base ** (
        -(jnp.arange(half_size, dtype=jnp.float32) * 2.0) / heads_in.shape[-1]
    )
    angles = positions.astype(jnp.float32)[:, None] * frequency[None, :]
    cosine = jnp.cos(angles)[:, None, :]
    sine_part = jnp.sin(angles)[:, None, :]
    first_half = heads_in[..., :half_size]
    second_half = heads_in[..., half_size:]
    return jnp.concatenate(
        [
            first_half * cosine - second_half * sine_part,
            second_half * cosine + first_half * sine_part,
        ],
        axis=-1,
    )


def visible(positions, length):
    query_ids = positions[:, None]
    key_ids = positions[None, :]
    real_key = (key_ids < MEM) | (key_ids - MEM < length)
    ordered = (key_ids <= query_ids) | (query_ids < MEM)
    return real_key & ordered


def normalize(widened, gain_row):
    scaled = widened * lax.rsqrt(jnp.mean(widened * widened, axis=-1, keepdims=True) + eps)
    return (scaled * gain_row).astype(jnp.bfloat16)


def attend(queries, key_heads, value_heads, positions, length):
    row_total = queries.shape[0]
    kv_local = key_heads.shape[1]
    grouped = queries.reshape(row_total, kv_local, -1, queries.shape[-1])
    scores = jnp.einsum(
        "qgrd,kgd->grqk", grouped, key_heads, preferred_element_type=jnp.float32
    ) * HD ** (-0.5)
    scores = jnp.where(visible(positions, length)[None, None], scores, -1e30)
    softmaxed = jax.nn.softmax(scores, axis=-1).astype(jnp.bfloat16)
    mixed = jnp.einsum(
        "grqk,kgd->qgrd", softmaxed, value_heads, preferred_element_type=jnp.float32
    ).astype(jnp.bfloat16)
    return mixed.reshape(row_total, -1)


def finish(widened, summed_out, length, row_ids):
    new_state = (widened + summed_out).astype(jnp.bfloat16)
    kept_rows = (row_ids < MEM) | (row_ids - MEM < length)
    return jnp.where(kept_rows[:, None], new_state, jnp.zeros_like(new_state))


def order_pair(mine, partner, lower_half):
    first_part = jnp.where(lower_half, mine, partner)
    second_part = jnp.where(lower_half, partner, mine)
    return jnp.concatenate([first_part, second_part], axis=0)


def gather_rows(piece, my_rank, seq_bits, rank_bits, level_list):
    stacked = piece
    for rank_bit in level_list:
        partner = from_partner(stacked, "tp", seq_bits + rank_bit)
        upper_half = my_rank // 2**rank_bit % 2 == 1
        stacked = jnp.where(
            upper_half, jnp.stack([partner, stacked], axis=0), jnp.stack([stacked, partner], axis=0)
        )
    axis_bits = list(reversed(level_list))
    order_axes = [axis_bits.index(rank_bit) for rank_bit in reversed(range(rank_bits))]
    stacked = jnp.transpose(stacked, order_axes + [rank_bits, rank_bits + 1])
    return stacked.reshape(2**rank_bits * piece.shape[0], piece.shape[-1])


def scatter_rows(partial_term, my_rank, seq_bits, rank_bits, level_list, shard_rows):
    model_width = partial_term.shape[-1]
    running = partial_term.reshape((2,) * rank_bits + (shard_rows, model_width))
    axis_bits = list(reversed(range(rank_bits)))
    for rank_bit in level_list:
        position = axis_bits.index(rank_bit)
        upper_half = my_rank // 2**rank_bit % 2 == 1
        low_part = lax.index_in_dim(running, 0, position, keepdims=False)
        high_part = lax.index_in_dim(running, 1, position, keepdims=False)
        kept_rows = jnp.where(upper_half, high_part, low_part)
        sent_rows = jnp.where(upper_half, low_part, high_part)
        running = kept_rows + from_partner(
            sent_rows.astype(jnp.bfloat16), "tp", seq_bits + rank_bit
        ).astype(sent_rows.dtype)
        axis_bits = [other_bit for other_bit in axis_bits if other_bit != rank_bit]
    return running


def local(embeddings, lengths, mem_init, norm_gain, w_query, w_key, w_value, w_out):
    axis_width = lax.axis_size("tp")
    group_size = axis_width // SECTIONS
    rank_count = min(8, group_size)
    seq_count = group_size // rank_count
    seq_bits = seq_count.bit_length() - 1
    rank_bits = rank_count.bit_length() - 1
    device_index = lax.axis_index("tp")
    group_index = device_index // group_size
    my_rank = device_index % group_size // seq_count
    my_seq = device_index % seq_count
    model_width = embeddings.shape[-1]
    row_total = SEG + MEM
    shard_rows = row_total // rank_count
    mem_block = MEM // rank_count
    token_block = SEG // rank_count
    within = jnp.arange(shard_rows, dtype=jnp.int32)
    block_ids = jnp.arange(rank_count, dtype=jnp.int32)[:, None]
    positions = jnp.where(
        within[None, :] < mem_block,
        block_ids * mem_block + within[None, :],
        MEM + block_ids * token_block + within[None, :] - mem_block,
    ).reshape(-1)
    row_ids = lax.dynamic_index_in_dim(
        positions.reshape(rank_count, shard_rows), my_rank, 0, keepdims=False
    )
    gain_row = lax.dynamic_index_in_dim(norm_gain, group_index, 0, keepdims=False)
    my_lengths = lax.dynamic_index_in_dim(lengths, my_seq, 0, keepdims=False)
    first_memory = lax.dynamic_slice(
        mem_init, (group_index, my_rank * mem_block, 0), (1, mem_block, model_width)
    ).reshape(mem_block, model_width)
    query_stack, key_stack, value_stack, out_stack = (
        w_query[None],
        w_key[None],
        w_value[None],
        w_out[None],
    )
    for seq_bit in range(seq_bits):
        partner_query, partner_key, partner_value, partner_out = (
            from_partner(shortened(query_stack), "tp", seq_bit).astype(query_stack.dtype),
            from_partner(shortened(key_stack), "tp", seq_bit).astype(key_stack.dtype),
            from_partner(shortened(value_stack), "tp", seq_bit).astype(value_stack.dtype),
            from_partner(shortened(out_stack), "tp", seq_bit).astype(out_stack.dtype),
        )
        lower_half = device_index // 2**seq_bit % 2 == 0
        query_stack = order_pair(query_stack, partner_query, lower_half)
        key_stack = order_pair(key_stack, partner_key, lower_half)
        value_stack = order_pair(value_stack, partner_value, lower_half)
        out_stack = order_pair(out_stack, partner_out, lower_half)
    level_list = list(range(rank_bits))
    states = jnp.zeros((SEGS, shard_rows, model_width), jnp.bfloat16)
    memory = jnp.zeros((mem_block, model_width), jnp.bfloat16)
    arrived = jnp.zeros((token_block, model_width), jnp.bfloat16)
    step_total = SEGS + SECTIONS - 1
    for step_index in range(step_total):
        segment = step_index - group_index
        active = (segment >= 0) & (segment < SEGS)
        clipped = jnp.clip(segment, 0, SEGS - 1)
        length = lax.dynamic_index_in_dim(my_lengths, clipped, 0, keepdims=False)
        embedded = lax.dynamic_slice(
            embeddings,
            (my_seq, clipped, my_rank * token_block, 0),
            (1, 1, token_block, model_width),
        ).reshape(token_block, model_width)
        token_source = jnp.where(group_index == 0, embedded, arrived)
        memory_source = jnp.where(segment == 0, first_memory, memory)
        inputs = jnp.concatenate([memory_source, token_source], axis=0)
        widened = inputs.astype(jnp.float32)
        normed = normalize(widened, gain_row)
        gathered = gather_rows(normed, my_rank, seq_bits, rank_bits, level_list)
        query_all = jnp.einsum(
            "rd,sdc->rsc", gathered, query_stack, preferred_element_type=jnp.float32
        )
        queries = rotate(query_all.reshape(row_total, -1, HD), positions).astype(jnp.bfloat16)
        key_all = jnp.einsum("rd,sdc->rsc", gathered, key_stack, preferred_element_type=jnp.float32)
        key_raw = lax.optimization_barrier(key_all.reshape(row_total, -1).astype(jnp.bfloat16))
        value_all = jnp.einsum(
            "rd,sdc->rsc", gathered, value_stack, preferred_element_type=jnp.float32
        ).astype(jnp.bfloat16)
        key_heads = rotate(
            key_raw.astype(jnp.float32).reshape(row_total, -1, HD), positions
        ).astype(jnp.bfloat16)
        value_heads = value_all.reshape(row_total, -1, HD)
        mixed_heads = attend(queries, key_heads, value_heads, positions, length)
        mixed_split = mixed_heads.reshape(row_total, out_stack.shape[0], out_stack.shape[1])
        partial_term = jnp.einsum(
            "rsc,scd->rd", mixed_split, out_stack, preferred_element_type=jnp.float32
        )
        summed_out = scatter_rows(
            partial_term, my_rank, seq_bits, rank_bits, level_list, shard_rows
        )
        new_state = finish(widened, summed_out, length, row_ids)
        memory = jnp.where(active, new_state[:mem_block], memory)
        states = jnp.where(
            active, lax.dynamic_update_index_in_dim(states, new_state, clipped, 0), states
        )
        if step_index + 1 < step_total:
            arrived = shifted(new_state[mem_block:], "tp", group_size)
    return states[None]


RANKS = 4
WIDTHS = (512, 512, 512, 512)
STARTS = tuple(sum(WIDTHS[:j]) for j in range(len(WIDTHS)))
CHUNKS = len(WIDTHS)
ROWS = SEG + MEM
GATHER = ('x0', 'g0', 'x1', 'g1', 'x2', 'h0', 'g2', 'x3', 'h1', 'g3', 'h2', 'h3')
FINISH = ('p0', 'o0', 'p1', 'o1', 'c0', 'p2', 'o2', 'c1', 'p3', 'o3', 'c2:4', 'm0:2', 'm2:4', 'e0', 't0:4', 'z0:4', 'f0:2', 'f2:4')


LATE = {2: range(2), 3: range(2, 4), 4: range(4, 6), 5: range(6, 8)}


def span(step):
    low, high = step[1:].split(":") if ":" in step else (step[1:], int(step[1:]) + 1)
    return int(low), int(high)


HALF_TOKENS = SEG // 2
HALF_MEM = MEM // 2
MESH = pl.DeviceIdType.MESH


def rope_tables(head):
    half = head // 2
    frequency = rope_base ** (-(np.arange(half, dtype=np.float64) * 2.0) / head)
    angles = np.arange(ROWS)[:, None] * frequency[None, :]
    cosine, sine = np.cos(angles), np.sin(angles)
    return (
        np.concatenate([cosine, cosine], axis=1).astype(np.float32),
        np.concatenate([-sine, sine], axis=1).astype(np.float32),
    )


def layer_kernel(
    len_ref, gain_ref, cos_ref, sin_ref, m0_ref, emb_ref, wq_ref, wk_ref, wv_ref, wo_ref,
    out_ref,
    wq_v, wk_v, wv_v, wo_v, xin, core_snd, core_rcv, tok_snd, tok_rcv, mem_snd, mem_rcv, newt,
    part, acc, mixed, gain_v, cos_v, sin_v,
    msem, esem, wsem, osem, ssem, send_sem, recv_sem,
):
    width = xin.shape[-1]
    half = width // 2
    q_cols, kv_cols = wq_v.shape[1], wk_v.shape[1]
    me = lax.axis_index("tp")
    group, rank = me // RANKS, me % RANKS
    xb, cb = rank // 2, rank % 2
    core_peer = group * RANKS + xb * 2 + (1 - cb)
    x_peer = group * RANKS + (1 - xb) * 2 + (1 - cb)
    has_next, has_prev = group < SECTIONS - 1, group > 0
    next_peer, prev_peer = me + RANKS, me - RANKS
    side = (rank // 2 + rank % 2) % 2
    own_rows = pl.ds(pl.multiple_of(MEM + xb * HALF_TOKENS, 16), HALF_TOKENS)
    far_rows = pl.ds(pl.multiple_of(MEM + (1 - xb) * HALF_TOKENS, 16), HALF_TOKENS)
    mem_rows = pl.ds(0, MEM)
    own_memory = pl.ds(pl.multiple_of(xb * HALF_MEM, 16), HALF_MEM)
    far_memory = pl.ds(pl.multiple_of((1 - xb) * HALF_MEM, 16), HALF_MEM)

    def reach(low, high=None):
        return STARTS[low], sum(WIDTHS[low : low + 1 if high is None else high])

    def own_cols(low, high=None):
        start, size = reach(low, high)
        return pl.ds(pl.multiple_of(side * half + start, 128), size)

    def peer_cols(low, high=None):
        start, size = reach(low, high)
        return pl.ds(pl.multiple_of((1 - side) * half + start, 128), size)

    def half_cols(low, high=None):
        return pl.ds(*reach(low, high))

    blocks_in = [(step[0] == "g", *span(step)) for step in GATHER if step[0] in "gh"]
    blocks_out = [(step[0] == "o", *span(step)) for step in FINISH if step[0] in "po"]
    memory_spans = dict(span(step) for step in FINISH if step[0] == "m")
    peer_out = {low: high for mine, low, high in blocks_out if not mine}

    def block_cols(mine, low, high):
        return own_cols(low, high) if mine else peer_cols(low, high)

    def weight_copies(o):
        cols = block_cols(*blocks_in[o])
        return [
            pltpu.make_async_copy(src.at[cols], dst.at[cols], wsem.at[i, o])
            for i, (src, dst) in enumerate(((wq_ref, wq_v), (wk_ref, wk_v), (wv_ref, wv_v)))
        ]

    def out_copy(o):
        cols = block_cols(*blocks_out[o])
        return pltpu.make_async_copy(wo_ref.at[:, cols], wo_v.at[:, cols], osem.at[o])

    def in_copy(k):
        return pltpu.make_async_copy(
            emb_ref.at[0, k], xin.at[k, pl.ds(MEM, SEG)], esem.at[k]
        )

    def remote(src, dst, kind, k, j, peer):
        return pltpu.make_async_remote_copy(
            src_ref=src, dst_ref=dst, send_sem=send_sem.at[kind, k, j],
            recv_sem=recv_sem.at[kind, k, j],
            device_id={"tp": peer}, device_id_type=MESH,
        )

    def in_place(ref, kind, k, j, peer):
        return remote(ref, ref, kind, k, j, peer)

    def z_copy(k, j):
        return remote(
            newt.at[k, :, own_cols(j)], xin.at[k, own_rows, own_cols(j)], 0, k, j, next_peer
        )

    def gather_x(k, j):
        return in_place(xin.at[k, own_rows, own_cols(j)], 1, k, j, x_peer)

    def gather_core(k, j):
        return in_place(xin.at[k, own_rows, own_cols(j)], 2, k, j, core_peer)

    def gather_far(k, j):
        return in_place(xin.at[k, far_rows, own_cols(j)], 3, k, j, core_peer)

    def sum_core(k, low):
        cols = half_cols(low, peer_out[low])
        return remote(core_snd.at[k, :, cols], core_rcv.at[k, :, cols], 4, k, low, core_peer)

    def sum_tokens(k, j):
        return remote(
            tok_snd.at[k, :, half_cols(j)], tok_rcv.at[k, :, half_cols(j)], 5, k, j, x_peer
        )

    def sum_memory(k, low):
        cols = half_cols(low, memory_spans[low])
        return remote(mem_snd.at[k, :, cols], mem_rcv.at[k, :, cols], 6, k, low, x_peer)

    def sum_last_memory(low):
        rows = (SEGS - 1, far_memory, half_cols(low, memory_spans[low]))
        return remote(mem_snd.at[*rows], mem_rcv.at[*rows], 6, SEGS - 1, low, x_peer)

    def last_memory(low):
        cols = own_cols(low, memory_spans[low])
        return in_place(xin.at[SEGS, own_memory, cols], 7, SEGS - 1, low, core_peer)

    def next_memory(k, low):
        cols = own_cols(low, memory_spans[low])
        return in_place(xin.at[k + 1, mem_rows, cols], 7, k, low, core_peer)

    def out_tokens(k):
        return in_place(newt.at[k, :, own_cols(0, CHUNKS)], 8, k, 0, core_peer)

    first_memory = pltpu.make_async_copy(m0_ref.at[group], xin.at[0, mem_rows], msem)
    gain_copy = pltpu.make_async_copy(gain_ref, gain_v, ssem.at[0])
    cos_copy = pltpu.make_async_copy(cos_ref, cos_v, ssem.at[1])
    sin_copy = pltpu.make_async_copy(sin_ref, sin_v, ssem.at[2])

    def start_weights(o):
        for copy in weight_copies(o):
            copy.start()

    @pl.when(group == 0)
    def _():
        in_copy(0).start()

    first_memory.start()
    gain_copy.start()
    start_weights(0)
    start_weights(1)

    barrier = pltpu.get_barrier_semaphore()
    for peer in (core_peer, x_peer):
        pl.semaphore_signal(barrier, inc=1, device_id={"tp": peer}, device_id_type=MESH)

    @pl.when(has_next)
    def _():
        pl.semaphore_signal(barrier, inc=1, device_id={"tp": next_peer}, device_id_type=MESH)

    @pl.when(has_prev)
    def _():
        pl.semaphore_signal(barrier, inc=1, device_id={"tp": prev_peer}, device_id_type=MESH)

    for o in range(2, len(blocks_in)):
        start_weights(o)
    cos_copy.start()
    sin_copy.start()

    @pl.when(has_prev)
    def _():
        for o in range(len(blocks_out)):
            out_copy(o).start()

    inner = has_next & has_prev

    @pl.when(inner)
    def _():
        pl.semaphore_wait(barrier, 4)

    @pl.when(has_prev & jnp.logical_not(has_next))
    def _():
        pl.semaphore_wait(barrier, 3)

    first_memory.wait()
    gain_copy.wait()

    def pass_on(k, j):
        @pl.when(has_prev)
        def _():
            z_copy(k, j).wait_recv()
            gather_x(k, j).start()
            gather_core(k, j).start()

    def pass_far(k, j):
        @pl.when(has_prev)
        def _():
            gather_x(k, j).wait_recv()
            gather_far(k, j).start()

    def rope(block):
        return block * cos_v[...] + pltpu.roll(block, HD // 2, 1) * sin_v[...]

    def emit_out(k, part_side):
        length = len_ref[0, k]
        step = half // 4
        row = lax.broadcasted_iota(jnp.int32, (32, step), 0)
        kept = (row < 8) | (xb * HALF_TOKENS + cb * 24 + row - 8 < length)
        for j in range(4):
            cols = pl.ds(pl.multiple_of(part_side * half + j * step, 128), step)
            memory = xin[k + 1, mem_rows, cols].astype(jnp.float32)
            tokens = newt[k, :, cols].astype(jnp.float32)
            low = jnp.where(xb == 0, memory[:16], memory[16:])
            block = jnp.concatenate(
                [
                    jnp.where(cb == 0, low[:8], low[8:]),
                    jnp.where(cb == 0, tokens[:24], tokens[24:]),
                ],
                axis=0,
            )
            out_ref[0, k, :, cols] = jnp.where(kept, block, 0.0).astype(jnp.bfloat16)

    def segment(k, carry):
        length = len_ref[0, k]
        squares = jnp.zeros((ROWS, 1), jnp.float32)

        @pl.when(group == 0)
        def _():
            in_copy(k).wait()

        o = 0
        for step in GATHER:
            kind, (j, last) = step[0], span(step)
            if kind == "z":
                pass_on(k, j)
                continue
            if kind == "x":
                pass_far(k, j)
                continue
            if kind == "h":

                @pl.when(has_prev)
                def _():
                    for i in range(j, last):
                        gather_core(k, i).wait_recv()
                        gather_far(k, i).wait_recv()

                @pl.when(k > 0)
                def _():
                    for i in range(j, last):
                        if i in memory_spans:
                            next_memory(k - 1, i).wait_recv()

            @pl.when(k == 0)
            def _():
                for copy in weight_copies(o):
                    copy.wait()

            if o in LATE:

                @pl.when((k == 0) & (group == 0))
                def _():
                    for i in LATE[o]:
                        out_copy(i).start()
                    if o == max(LATE):
                        for i in range(1, SEGS):
                            in_copy(i).start()

            cols = block_cols(*blocks_in[o])
            raw = xin[k, :, cols].astype(jnp.float32)
            squares = squares + jnp.sum(raw * raw, axis=1, keepdims=True)
            gained = (raw * gain_v[pl.ds(group, 1), cols]).astype(jnp.bfloat16)
            low = 0
            for weight in (wq_v, wk_v, wv_v):
                high = low + weight.shape[1]
                term = jnp.dot(gained, weight[cols], preferred_element_type=jnp.float32)
                if o == 0:
                    acc[:, low:high] = term
                else:
                    acc[:, low:high] += term
                low = high
            o += 1

        @pl.when(k == 0)
        def _():
            cos_copy.wait()
            sin_copy.wait()

        @pl.when((k == 0) & (group == 0))
        def _():
            pl.semaphore_wait(barrier, 3)

        factor = lax.rsqrt(squares * (1.0 / width) + eps)
        query_pos = lax.broadcasted_iota(jnp.int32, (ROWS, ROWS), 0)
        key_pos = lax.broadcasted_iota(jnp.int32, (ROWS, ROWS), 1)
        real_key = (key_pos < MEM) | (key_pos - MEM < length)
        ordered = (key_pos <= query_pos) | (query_pos < MEM)
        bias = jnp.where(real_key & ordered, 0.0, -1e30).astype(jnp.float32)
        per_kv = q_cols // kv_cols
        for g in range(kv_cols // HD):
            key_raw = (acc[:, q_cols + g * HD : q_cols + (g + 1) * HD] * factor).astype(
                jnp.bfloat16
            )
            key = rope(key_raw.astype(jnp.float32)).astype(jnp.bfloat16)
            low = q_cols + kv_cols + g * HD
            value = (acc[:, low : low + HD] * factor).astype(jnp.bfloat16)
            heads = range(g * per_kv, (g + 1) * per_kv)
            queries = jnp.concatenate(
                [
                    rope(acc[:, h * HD : (h + 1) * HD] * factor).astype(jnp.bfloat16)
                    for h in heads
                ],
                axis=0,
            )
            scores = lax.dot_general(
                queries, key, (((1,), (1,)), ((), ())), preferred_element_type=jnp.float32
            ) * HD ** (-0.5)
            scores = scores.reshape(per_kv, ROWS, ROWS) + bias[None]
            weight = jnp.exp(scores - jnp.max(scores, axis=2, keepdims=True))
            share = 1.0 / jnp.sum(weight, axis=2, keepdims=True)
            blended = jnp.dot(
                weight.astype(jnp.bfloat16).reshape(per_kv * ROWS, ROWS),
                value,
                preferred_element_type=jnp.float32,
            ).reshape(per_kv, ROWS, HD) * share
            for i, h in enumerate(heads):
                mixed[:, h * HD : (h + 1) * HD] = blended[i].astype(jnp.bfloat16)

        def project_peer(low, high):
            @pl.when(k == 0)
            def _():
                out_copy(blocks_out.index((False, low, high))).wait()

            term = jnp.dot(
                mixed[...], wo_v[:, peer_cols(low, high)], preferred_element_type=jnp.float32
            )
            core_snd[k, :, half_cols(low, high)] = term.astype(jnp.bfloat16)
            sum_core(k, low).start()

        def project_own(low, high):
            @pl.when(k == 0)
            def _():
                out_copy(blocks_out.index((True, low, high))).wait()

            part[:, half_cols(low, high)] = jnp.dot(
                mixed[...], wo_v[:, own_cols(low, high)], preferred_element_type=jnp.float32
            )

        def cross(j):
            if j in peer_out:
                sum_core(k, j).wait_recv()
            cols = half_cols(j)
            far = part[far_rows, cols] + core_rcv[k, far_rows, cols].astype(jnp.float32)
            tok_snd[k, :, cols] = far.astype(jnp.bfloat16)
            sum_tokens(k, j).start()
            part[own_rows, cols] = (
                part[own_rows, cols]
                + core_rcv[k, own_rows, cols].astype(jnp.float32)
                + xin[k, own_rows, own_cols(j)].astype(jnp.float32)
            )

        def cross_memory(low, high):
            cols = half_cols(low, high)
            memory = part[mem_rows, cols] + core_rcv[k, mem_rows, cols].astype(jnp.float32)
            mem_snd[k, :, cols] = memory.astype(jnp.bfloat16)

            @pl.when(k + 1 < SEGS)
            def _():
                sum_memory(k, low).start()

            @pl.when(k + 1 == SEGS)
            def _():
                sum_last_memory(low).start()

            part[mem_rows, cols] = memory + xin[k, mem_rows, own_cols(low, high)].astype(jnp.float32)

        def finish_tokens(j):
            sum_tokens(k, j).wait_recv()
            cols = half_cols(j)
            state = part[own_rows, cols] + tok_rcv[k, :, cols].astype(jnp.float32)
            newt[k, :, own_cols(j)] = state.astype(jnp.bfloat16)

            @pl.when(has_next)
            def _():
                z_copy(k, j).start()

            if j == CHUNKS - 1:
                out_tokens(k).start()

        def finish_memory(low, high):
            cols = half_cols(low, high)

            @pl.when(k + 1 < SEGS)
            def _():
                sum_memory(k, low).wait_recv()
                state = part[mem_rows, cols] + mem_rcv[k, :, cols].astype(jnp.float32)
                xin[k + 1, mem_rows, own_cols(low, high)] = state.astype(jnp.bfloat16)
                next_memory(k, low).start()

            @pl.when(k + 1 == SEGS)
            def _():
                sum_last_memory(low).wait_recv()
                got = mem_rcv[SEGS - 1, own_memory, cols].astype(jnp.float32)
                state = part[own_memory, cols] + got
                xin[SEGS, own_memory, own_cols(low, high)] = state.astype(jnp.bfloat16)
                last_memory(low).start()

        def emit_last(j):
            @pl.when(k > 0)
            def _():
                out_tokens(k - 1).wait_recv()
                emit_out(k - 1, side)
                emit_out(k - 1, 1 - side)

        def pass_next(j):
            @pl.when(k + 1 < SEGS)
            def _():
                pass_on(k + 1, j)

        def pass_far_next(j):
            @pl.when(k + 1 < SEGS)
            def _():
                pass_far(k + 1, j)

        actions = {
            "p": project_peer, "o": project_own, "c": cross, "m": cross_memory,
            "t": finish_tokens, "f": finish_memory, "e": emit_last, "z": pass_next,
            "x": pass_far_next,
        }
        for step in FINISH:
            if step[0] in "pomf":
                actions[step[0]](*span(step))
            else:
                for j in range(*span(step)):
                    actions[step[0]](j)
        return carry

    for j in range(CHUNKS):
        pass_on(0, j)
    lax.fori_loop(0, SEGS, segment, 0)
    emit_out(SEGS - 1, side)
    out_tokens(SEGS - 1).wait_recv()
    for low in memory_spans:
        last_memory(low).wait_recv()
    emit_out(SEGS - 1, 1 - side)

    def drain(k, carry):
        for low in peer_out:
            sum_core(k, low).wait_send()
        out_tokens(k).wait_send()
        for low in memory_spans:

            @pl.when(k + 1 < SEGS)
            def _():
                sum_memory(k, low).wait_send()
                next_memory(k, low).wait_send()

            @pl.when(k + 1 == SEGS)
            def _():
                sum_last_memory(low).wait_send()
                last_memory(low).wait_send()

        for j in range(CHUNKS):
            sum_tokens(k, j).wait_send()

            @pl.when(has_next)
            def _():
                z_copy(k, j).wait_send()

            @pl.when(has_prev)
            def _():
                gather_x(k, j).wait_send()
                gather_core(k, j).wait_send()
                gather_far(k, j).wait_send()


        return carry

    lax.fori_loop(0, SEGS, drain, 0)


def streamed(embeddings, lengths, mem_init, norm_gain, w_query, w_key, w_value, w_out):
    width = embeddings.shape[-1]
    q_cols, kv_cols = w_query.shape[1], w_key.shape[1]
    cosine, sine = rope_tables(HD)
    anywhere = pl.BlockSpec(memory_space=pl.ANY)
    dma = pltpu.SemaphoreType.DMA
    half = jnp.bfloat16
    return pl.pallas_call(
        layer_kernel,
        out_shape=pltpu.VMEM((1, SEGS, 32, width), half),
        in_specs=[pl.BlockSpec(memory_space=pltpu.SMEM)] + [anywhere] * 9,
        out_specs=pl.BlockSpec(memory_space=pltpu.VMEM),
        scratch_shapes=[
            pltpu.VMEM((width, q_cols), half),
            pltpu.VMEM((width, kv_cols), half),
            pltpu.VMEM((width, kv_cols), half),
            pltpu.VMEM((q_cols, width), half),
            pltpu.VMEM((SEGS + 1, ROWS, width), half),
            pltpu.VMEM((SEGS, ROWS, width // 2), half),
            pltpu.VMEM((SEGS, ROWS, width // 2), half),
            pltpu.VMEM((SEGS, HALF_TOKENS, width // 2), half),
            pltpu.VMEM((SEGS, HALF_TOKENS, width // 2), half),
            pltpu.VMEM((SEGS, MEM, width // 2), half),
            pltpu.VMEM((SEGS, MEM, width // 2), half),
            pltpu.VMEM((SEGS, HALF_TOKENS, width), half),
            pltpu.VMEM((ROWS, width // 2), jnp.float32),
            pltpu.VMEM((ROWS, q_cols + 2 * kv_cols), jnp.float32),
            pltpu.VMEM((ROWS, q_cols), half),
            pltpu.VMEM(norm_gain.shape, jnp.float32),
            pltpu.VMEM((ROWS, HD), jnp.float32),
            pltpu.VMEM((ROWS, HD), jnp.float32),
            dma,
            dma((SEGS,)),
            dma((3, 2 * CHUNKS)),
            dma((2 * CHUNKS,)),
            dma((3,)),
            dma((9, SEGS, CHUNKS)),
            dma((9, SEGS, CHUNKS)),
        ],
        compiler_params=pltpu.CompilerParams(
            collective_id=0, has_side_effects=True, vmem_limit_bytes=56 * 2**20
        ),
    )(
        lengths, norm_gain, jnp.asarray(cosine), jnp.asarray(sine), mem_init, embeddings,
        w_query, w_key, w_value, w_out,
    )


def solution(mesh):
    in_specs = (
        P("parts", None, None, None),
        P("parts", None),
        P(),
        P(),
        P(None, "tp"),
        P(None, "tp"),
        P(None, "tp"),
        P("tp", None),
    )
    out_specs = P("tp", "parts", None, None)
    body = streamed if mesh.shape["tp"] == SECTIONS * RANKS else local
    return jax.shard_map(body, mesh=mesh, in_specs=in_specs, out_specs=out_specs, check_vma=False)
```
